1024 devices in a mesh: px: 8 (over y), py: 64 (over x_hi, z, core), lev: 2 (over x_lo).
Axes of the slice: x: 8 (x_hi: 4, x_lo: 2; x = x_hi * 2 + x_lo), y: 8, z: 8, core: 2. Of those that a mesh axis runs over, the one named last changes fastest.
Arguments:
- tracer: float32 [2, 8, 64, 8192], P('lev', None, 'px', 'py'), may hold values from -6 to 6
- node_mass: float32 [2, 64, 8192], P('lev', 'px', 'py'), may hold values from 0.5 to 2
- wind_x: float32 [2, 64, 8192], P('lev', 'px', 'py'), may hold values from -4 to 4
- wind_y: float32 [2, 64, 8192], P('lev', 'px', 'py'), may hold values from -4 to 4
- remap: float32 [2, 2], replicated, may hold values from -4 to 4
Outputs:
- remapped: float32 [2, 8, 64, 8192], P(None, 'lev', 'px', 'py')
The draws below stay inside these ranges and needn't reach their ends.
All inputs are finite; a program needn't handle non-finite values.
Results may differ from the reference program's by a relative error of at most 0.0001.
Values sent between devices are 32-bit elements; how exact they have to be, the bound alone decides.
No kernel may reach another device: no remote copies, remote signals or barrier semaphores. Data moves between devices by JAX's collectives and lax.ppermute only.
A program may use at most 32 MiB of HBM per device.

```python
import math
import jax
import jax.numpy as jnp
import numpy as np
from jax import lax

GLL_NODES = 4
TRACERS = 8
LEVELS = 2
GRID_X = 64
GRID_Y = 8192


def level_of(rng, extent, pieces, least, high):
    def one(position, blocks):
        heights = jax.random.uniform(jax.random.fold_in(jax.random.fold_in(rng, 6), position), (blocks,), jnp.float32, least / len(pieces), high / len(pieces))
        return jnp.repeat(jnp.exp(heights), extent[position] // blocks).reshape((-1,) + (1,) * (len(extent) - position - 1))

    loudness = one(*pieces[0])
    for cut in pieces[1:]:
        loudness = loudness * one(*cut)
    return loudness


def centred(rng, dims, scale, reach, split=(), dtype=jnp.bfloat16):
    gain = level_of(rng, dims, split, -0.22, 0.18) if split else 1.0
    values = jax.random.normal(rng, dims, jnp.float32) * scale * gain
    return jnp.minimum(jnp.maximum(values, -reach), reach).astype(dtype)


def setup_inputs(seed: int = 0) -> dict:
    key_list = jax.random.split(jax.random.key(seed), 6)
    return {
        "tracer": centred(key_list[0], (LEVELS, TRACERS, GRID_X, GRID_Y), 1.0, 6.0, ((0, 2), (2, 8), (3, 64)), jnp.float32),
        "node_mass": jnp.clip(jnp.exp(math.log(2.0) - 1.3862944 * jax.random.uniform(key_list[1], (LEVELS, GRID_X, GRID_Y), jnp.float32) ** level_of(key_list[1], (LEVELS, GRID_X, GRID_Y), ((0, 2), (1, 8), (2, 64)), -0.2, 0.2)), 0.5, 2.0),
        "wind_x": centred(key_list[2], (LEVELS, GRID_X, GRID_Y), 1.0, 4.0, ((0, 2), (1, 8), (2, 64)), jnp.float32),
        "wind_y": centred(key_list[3], (LEVELS, GRID_X, GRID_Y), 1.0, 4.0, ((0, 2), (1, 8), (2, 64)), jnp.float32),
        "remap": centred(key_list[4], (LEVELS, LEVELS), LEVELS ** -0.5, 4.0, (), jnp.float32),
    }


sentinel = 1.0e30
step_size = 0.1
section_weights = ((0.0, 1.0), (0.75, 0.25), (1.0 / 3.0, 2.0 / 3.0))


def derivative_table():
    points = np.array([-1.0, -(5.0 ** -0.5), 5.0 ** -0.5, 1.0])
    number = points.shape[0]
    barycentric = np.array([1.0 / np.prod([points[outer] - points[inner] for inner in range(number) if inner != outer]) for outer in range(number)])
    table = np.zeros((number, number))
    for outer in range(number):
        for inner in range(number):
            if inner != outer:
                table[outer, inner] = barycentric[inner] / barycentric[outer] / (points[outer] - points[inner])
    for outer in range(number):
        table[outer, outer] = -np.sum(table[outer])
    return table


def pair_sum(values, which_axis, cyclic):
    layout = values.shape
    where_at = len(layout) + which_axis
    elements = layout[where_at] // GLL_NODES
    blocked = values.reshape(layout[:where_at] + (elements, GLL_NODES) + layout[where_at + 1:])
    head_nodes = lax.slice_in_dim(blocked, 0, 1, axis=where_at + 1)
    tail_nodes = lax.slice_in_dim(blocked, GLL_NODES - 1, GLL_NODES, axis=where_at + 1)
    middle = lax.slice_in_dim(blocked, 1, GLL_NODES - 1, axis=where_at + 1)
    if cyclic:
        before = jnp.roll(tail_nodes, 1, axis=where_at)
        following = jnp.roll(head_nodes, -1, axis=where_at)
    else:
        zero_slab = jnp.zeros_like(lax.slice_in_dim(tail_nodes, 0, 1, axis=where_at))
        before = jnp.concatenate([zero_slab, lax.slice_in_dim(tail_nodes, 0, elements - 1, axis=where_at)], axis=where_at)
        following = jnp.concatenate([lax.slice_in_dim(head_nodes, 1, elements, axis=where_at), zero_slab], axis=where_at)
    joined = jnp.concatenate([head_nodes + before, middle, tail_nodes + following], axis=where_at + 1)
    return joined.reshape(layout)


def shared(values):
    return pair_sum(pair_sum(values, -2, True), -1, False)


def element_extrema(field):
    layout = field.shape
    blocked = field.reshape(layout[0], layout[1], layout[2] // GLL_NODES, GLL_NODES, layout[3] // GLL_NODES, GLL_NODES)
    return jnp.stack([jnp.min(blocked, axis=(3, 5)), -jnp.max(blocked, axis=(3, 5))])


def neighbourhood(padded):
    rows_min = jnp.minimum(jnp.minimum(padded[..., :-2, :], padded[..., 1:-1, :]), padded[..., 2:, :])
    return jnp.minimum(jnp.minimum(rows_min[..., :-2], rows_min[..., 1:-1]), rows_min[..., 2:])


def bounds(field):
    extrema = element_extrema(field)
    extrema = jnp.concatenate([extrema[..., -1:, :], extrema, extrema[..., :1, :]], axis=-2)
    extrema = jnp.pad(extrema, ((0, 0), (0, 0), (0, 0), (0, 0), (1, 1)), constant_values=sentinel)
    result = neighbourhood(extrema)
    return result[0], -result[1]


def tendency(field, wind_x, wind_y, table):
    layout = field.shape
    flux_x = (wind_x[:, None] * field).reshape(layout[0], layout[1], layout[2] // GLL_NODES, GLL_NODES, layout[3])
    slope_x = jnp.einsum("ij,lcejy->lceiy", table, flux_x, precision=lax.Precision.HIGHEST).reshape(layout)
    flux_y = (wind_y[:, None] * field).reshape(layout[0], layout[1], layout[2], layout[3] // GLL_NODES, GLL_NODES)
    slope_y = jnp.einsum("ij,lcxej->lcxei", table, flux_y, precision=lax.Precision.HIGHEST).reshape(layout)
    return field - step_size * (slope_x + slope_y)


def limit(moved, lower, upper):
    layout = moved.shape
    blocked = moved.reshape(layout[0], layout[1], layout[2] // GLL_NODES, GLL_NODES, layout[3] // GLL_NODES, GLL_NODES)
    clipped = jnp.clip(blocked, lower[:, :, :, None, :, None], upper[:, :, :, None, :, None])
    return clipped.reshape(layout)


def reference(tracer, node_mass, wind_x, wind_y, remap):
    table = jnp.asarray(derivative_table(), jnp.float32)
    mass_sum = shared(node_mass)

    def advance(column):
        start = column[:, None]
        field = start
        for share_start, share_new in section_weights:
            lower, upper = bounds(field)
            limited = limit(tendency(field, wind_x, wind_y, table), lower, upper)
            summed = shared(node_mass[:, None] * limited)
            field = share_start * start + share_new * (summed / mass_sum[:, None])
        return jnp.einsum("ab,bxy->axy", remap, field[:, 0], precision=lax.Precision.HIGHEST)

    columns = lax.map(advance, jnp.moveaxis(tracer, 1, 0))
    return jnp.moveaxis(columns, 0, 1)
```

```python
import functools

import jax
import jax.numpy as jnp
import numpy as np
from jax import lax
from jax.experimental import pallas as pl
from jax.experimental.pallas import tpu as pltpu
from jax.sharding import PartitionSpec as P

GLL_NODES = 4
LANES = 128
PARAMS = pltpu.CompilerParams(vmem_limit_bytes=8 * 1024 * 1024)
SLOT = 32

sentinel = 1e30
step_size = 0.1
section_weights = ((0.0, 1.0), (0.75, 0.25), (1.0 / 3.0, 2.0 / 3.0))


def derivative_table():
    points = np.array([-1.0, -(5.0 ** (-0.5)), 5.0 ** (-0.5), 1.0])
    number = points.shape[0]
    barycentric = np.array(
        [
            1.0
            / np.prod([points[outer] - points[inner] for inner in range(number) if inner != outer])
            for outer in range(number)
        ]
    )
    table = np.zeros((number, number))
    for outer in range(number):
        for inner in range(number):
            if inner != outer:
                table[outer, inner] = (
                    barycentric[inner] / barycentric[outer] / (points[outer] - points[inner])
                )
    for outer in range(number):
        table[outer, outer] = -np.sum(table[outer])
    return table


def rot(x, k):
    k = k % LANES
    return pltpu.roll(x, k, 1) if k else x


def lane_index():
    return lax.broadcasted_iota(jnp.int32, (8, LANES), 1)


def edges_kernel(r_ref, in_ref, cross_ref):
    slot = lane_index() // SLOT
    even = lax.axis_index("py") % 2 == 0
    for r in range(8):
        left = right = None
        for a in range(4):
            x = r_ref[:, a, r, :]
            lo, hi = rot(x, SLOT * a), rot(x, SLOT * a + SLOT)
            left = lo if a == 0 else jnp.where(slot == a, lo, left)
            right = hi if a == 0 else jnp.where(slot == a, hi, right)
        in_ref[r] = jnp.where(even, right, left)
        cross_ref[r] = jnp.where(even, left, right)


def sections_kernel(r_ref, in_ref, cross_ref, out_ref):
    lane = lane_index()
    node = lane % GLL_NODES
    py = lax.axis_index("py")
    even = py % 2 == 0
    has_left = py > 0
    has_right = py < lax.axis_size("py") - 1
    exists = ((lane < 64) & has_right) | ((lane >= 64) & has_left)
    table = derivative_table() * step_size
    rows = range(8)

    def pairs(a, fill):
        own, halo = [], []
        for r in rows:
            from_right = jnp.where(even, in_ref[r], cross_ref[r])
            from_left = jnp.where(even, cross_ref[r], in_ref[r])
            second = jnp.where(
                lane >= LANES - SLOT, rot(from_left, -SLOT * a - SLOT), jnp.float32(fill)
            )
            second = jnp.where(lane < SLOT, rot(from_right, -SLOT * a), second)
            own.append(r_ref[:, a, r, :])
            halo.append(second)
        return [own, halo]

    def before(f, k):
        o, h = rot(f[0], k), rot(f[1], k)
        return jnp.where(lane < k, h, o), jnp.where(lane < k, o, h)

    def after(f, k):
        o, h = rot(f[0], -k), rot(f[1], -k)
        return jnp.where(lane >= LANES - k, h, o), jnp.where(lane >= LANES - k, o, h)

    def up(x):
        return pltpu.roll(x, 1, 0)

    def down(x):
        return pltpu.roll(x, 7, 0)

    def shared(f):
        f = [list(part) for part in f]
        for part in f:
            first, last = part[0], part[7]
            part[0] = first + up(last)
            part[7] = last + down(first)
            part[3] = part[4] = part[3] + part[4]
        for r in rows:
            both = (f[0][r], f[1][r])
            lo, hi = before(both, 1), after(both, 1)
            for s in range(2):
                extra = jnp.where(node == 0, lo[s], jnp.where(node == 3, hi[s], 0.0))
                f[s][r] = both[s] + extra
        return f

    def extreme(f, op, missing):
        parts = []
        for s in range(2):
            halves = []
            for e in range(2):
                x = f[s][4 * e]
                for i in range(1, 4):
                    x = op(x, f[s][4 * e + i])
                x = op(x, jnp.where(lane % 2 == 1, rot(x, 1), rot(x, -1)))
                x = op(x, jnp.where(node >= 2, rot(x, 2), rot(x, -2)))
                if s == 1:
                    x = jnp.where(exists, x, missing)
                halves.append(x)
            zero, one = halves
            parts.append((op(op(zero, one), up(one)), op(op(zero, one), down(zero))))
        result = [[None, None], [None, None]]
        for e in range(2):
            both = (parts[0][e], parts[1][e])
            lo, hi = before(both, 4), after(both, 4)
            for s in range(2):
                result[s][e] = op(op(both[s], lo[s]), hi[s])
        return result

    coefficient = {}
    for k in range(-3, 4):
        c = jnp.zeros((8, LANES), jnp.float32)
        for i in range(4):
            if 0 <= i + k < 4:
                c = jnp.where(node == i, jnp.float32(table[i, i + k]), c)
        coefficient[k] = c

    start = pairs(0, 0.0)
    mass = pairs(1, 1.0)
    wind_x = pairs(2, 0.0)
    wind_y = pairs(3, 0.0)
    mass_sum = shared(mass)
    inverse = [
        [1.0 / m for m in mass_sum[0]],
        [jnp.where(exists, 1.0 / jnp.where(exists, m, 1.0), 0.0) for m in mass_sum[1]],
    ]
    field = start
    for share_start, share_new in section_weights:
        lower = extreme(field, jnp.minimum, sentinel)
        upper = extreme(field, jnp.maximum, -sentinel)
        weighted = [[None] * 8, [None] * 8]
        for s in range(2):
            for e in range(2):
                flux_x = [wind_x[s][4 * e + i] * field[s][4 * e + i] for i in range(4)]
                for i in range(4):
                    r = 4 * e + i
                    slope = jnp.float32(table[i, 0]) * flux_x[0]
                    for j in range(1, 4):
                        slope = slope + jnp.float32(table[i, j]) * flux_x[j]
                    flux_y = wind_y[s][r] * field[s][r]
                    for k in range(-3, 4):
                        slope = slope + coefficient[k] * rot(flux_y, -k)
                    moved = field[s][r] - slope
                    limited = jnp.minimum(jnp.maximum(moved, lower[s][e]), upper[s][e])
                    weighted[s][r] = mass[s][r] * limited
        summed = shared(weighted)
        fresh = [[None] * 8, [None] * 8]
        for s in range(2):
            for r in rows:
                value = jnp.float32(share_new) * (summed[s][r] * inverse[s][r])
                if share_start:
                    value = jnp.float32(share_start) * start[s][r] + value
                fresh[s][r] = value
        field = fresh
    for r in rows:
        out_ref[:, 0, r, :] = field[0][r]
        out_ref[:, 1, r, :] = field[0][r]


def remap_kernel(remap_ref, x_ref, out_ref):
    base = lax.axis_index("lev") * 8
    for t in range(4):
        low, high = x_ref[base + 2 * t], x_ref[base + 2 * t + 1]
        for level in range(2):
            out_ref[level, t] = remap_ref[level, 0] * low + remap_ref[level, 1] * high


def vmem(count):
    return [pl.BlockSpec(memory_space=pltpu.VMEM)] * count


def shards(tracer, node_mass, wind_x, wind_y, remap):
    count = lax.axis_size("py")
    common = jnp.stack([node_mass[0], wind_x[0], wind_y[0]])
    packed = jnp.concatenate(
        [tracer[0][:, None], jnp.broadcast_to(common[None], (8, 3, 8, LANES))], axis=1
    )
    rows = lax.all_to_all(packed, "px", 0, 0, tiled=True)
    edge = jax.ShapeDtypeStruct((8, 8, LANES), jnp.float32)
    inside, cross = pl.pallas_call(
        edges_kernel,
        out_shape=(edge, edge),
        in_specs=vmem(1),
        out_specs=tuple(vmem(2)),
        compiler_params=PARAMS,
        name="edges",
    )(rows)
    cross_pairs = [(i, i + 1 if i % 2 else i - 1) for i in range(1, count - 1)]
    inside_pairs = [(i, i ^ 1) for i in range(count)]
    cross = lax.ppermute(cross, "py", cross_pairs)
    inside = lax.ppermute(inside, "py", inside_pairs)
    done = pl.pallas_call(
        sections_kernel,
        out_shape=jax.ShapeDtypeStruct((8, 2, 8, LANES), jnp.float32),
        in_specs=vmem(3),
        out_specs=vmem(1)[0],
        compiler_params=PARAMS,
        name="sections",
    )(rows, inside, cross)
    back = lax.all_to_all(done.reshape(16, 8, LANES), ("px", "lev"), 0, 0, tiled=True)
    return pl.pallas_call(
        remap_kernel,
        out_shape=jax.ShapeDtypeStruct((2, 4, 8, LANES), jnp.float32),
        in_specs=[pl.BlockSpec(memory_space=pltpu.SMEM)] + vmem(1),
        out_specs=vmem(1)[0],
        compiler_params=PARAMS,
        name="remap",
    )(remap, back)


def solution(mesh):
    in_specs = (
        P("lev", None, "px", "py"),
        P("lev", "px", "py"),
        P("lev", "px", "py"),
        P("lev", "px", "py"),
        P(),
    )
    out_specs = P(None, "lev", "px", "py")
    return jax.shard_map(shards, mesh=mesh, in_specs=in_specs, out_specs=out_specs, check_vma=False)
```

```python
import jax
import jax.numpy as jnp
import numpy as np
from jax import lax
from jax.experimental import pallas as pl
from jax.experimental.pallas import tpu as pltpu
from jax.sharding import PartitionSpec as P


GLL_NODES = 4
LANES = 128
PARAMS = pltpu.CompilerParams(vmem_limit_bytes=8 * 1024 * 1024)
SLOT = 32

sentinel = 1e30
step_size = 0.1
section_weights = ((0.0, 1.0), (0.75, 0.25), (1.0 / 3.0, 2.0 / 3.0))


def derivative_table():
    points = np.array([-1.0, -(5.0 ** (-0.5)), 5.0 ** (-0.5), 1.0])
    number = points.shape[0]
    barycentric = np.array(
        [
            1.0
            / np.prod([points[outer] - points[inner] for inner in range(number) if inner != outer])
            for outer in range(number)
        ]
    )
    table = np.zeros((number, number))
    for outer in range(number):
        for inner in range(number):
            if inner != outer:
                table[outer, inner] = (
                    barycentric[inner] / barycentric[outer] / (points[outer] - points[inner])
                )
    for outer in range(number):
        table[outer, outer] = -np.sum(table[outer])
    return table


def rot(x, k):
    k = k % LANES
    return pltpu.roll(x, k, 1) if k else x


def lane_index():
    return lax.broadcasted_iota(jnp.int32, (8, LANES), 1)


def edges_kernel(r_ref, in_ref, cross_ref):
    slot = lane_index() // SLOT
    even = lax.axis_index("py") % 2 == 0
    for r in range(8):
        left = right = None
        for a in range(4):
            x = r_ref[:, a, r, :]
            lo, hi = rot(x, SLOT * a), rot(x, SLOT * a + SLOT)
            left = lo if a == 0 else jnp.where(slot == a, lo, left)
            right = hi if a == 0 else jnp.where(slot == a, hi, right)
        in_ref[r] = jnp.where(even, right, left)
        cross_ref[r] = jnp.where(even, left, right)


def sections_kernel(r_ref, in_ref, cross_ref, out_ref):
    lane = lane_index()
    node = lane % GLL_NODES
    py = lax.axis_index("py")
    even = py % 2 == 0
    has_left = py > 0
    has_right = py < lax.axis_size("py") - 1
    exists = ((lane < 64) & has_right) | ((lane >= 64) & has_left)
    table = derivative_table() * step_size
    rows = range(8)

    def pairs(a, fill):
        own, halo = [], []
        for r in rows:
            from_right = jnp.where(even, in_ref[r], cross_ref[r])
            from_left = jnp.where(even, cross_ref[r], in_ref[r])
            second = jnp.where(
                lane >= LANES - SLOT, rot(from_left, -SLOT * a - SLOT), jnp.float32(fill)
            )
            second = jnp.where(lane < SLOT, rot(from_right, -SLOT * a), second)
            own.append(r_ref[:, a, r, :])
            halo.append(second)
        return [own, halo]

    def before(f, k):
        o, h = rot(f[0], k), rot(f[1], k)
        return jnp.where(lane < k, h, o), jnp.where(lane < k, o, h)

    def after(f, k):
        o, h = rot(f[0], -k), rot(f[1], -k)
        return jnp.where(lane >= LANES - k, h, o), jnp.where(lane >= LANES - k, o, h)

    def up(x):
        return pltpu.roll(x, 1, 0)

    def down(x):
        return pltpu.roll(x, 7, 0)

    def shared(f):
        f = [list(part) for part in f]
        for part in f:
            first, last = part[0], part[7]
            part[0] = first + up(last)
            part[7] = last + down(first)
            part[3] = part[4] = part[3] + part[4]
        for r in rows:
            both = (f[0][r], f[1][r])
            lo, hi = before(both, 1), after(both, 1)
            for s in range(2):
                extra = jnp.where(node == 0, lo[s], jnp.where(node == 3, hi[s], 0.0))
                f[s][r] = both[s] + extra
        return f

    def extreme(f, op, missing):
        parts = []
        for s in range(2):
            halves = []
            for e in range(2):
                x = f[s][4 * e]
                for i in range(1, 4):
                    x = op(x, f[s][4 * e + i])
                x = op(x, jnp.where(lane % 2 == 1, rot(x, 1), rot(x, -1)))
                x = op(x, jnp.where(node >= 2, rot(x, 2), rot(x, -2)))
                if s == 1:
                    x = jnp.where(exists, x, missing)
                halves.append(x)
            zero, one = halves
            parts.append((op(op(zero, one), up(one)), op(op(zero, one), down(zero))))
        result = [[None, None], [None, None]]
        for e in range(2):
            both = (parts[0][e], parts[1][e])
            lo, hi = before(both, 4), after(both, 4)
            for s in range(2):
                result[s][e] = op(op(both[s], lo[s]), hi[s])
        return result

    coefficient = {}
    for k in range(-3, 4):
        c = jnp.zeros((8, LANES), jnp.float32)
        for i in range(4):
            if 0 <= i + k < 4:
                c = jnp.where(node == i, jnp.float32(table[i, i + k]), c)
        coefficient[k] = c

    start = pairs(0, 0.0)
    mass = pairs(1, 1.0)
    wind_x = pairs(2, 0.0)
    wind_y = pairs(3, 0.0)
    mass_sum = shared(mass)
    inverse = [
        [1.0 / m for m in mass_sum[0]],
        [jnp.where(exists, 1.0 / jnp.where(exists, m, 1.0), 0.0) for m in mass_sum[1]],
    ]
    field = start
    for share_start, share_new in section_weights:
        lower = extreme(field, jnp.minimum, sentinel)
        upper = extreme(field, jnp.maximum, -sentinel)
        weighted = [[None] * 8, [None] * 8]
        for s in range(2):
            for e in range(2):
                flux_x = [wind_x[s][4 * e + i] * field[s][4 * e + i] for i in range(4)]
                for i in range(4):
                    r = 4 * e + i
                    slope = jnp.float32(table[i, 0]) * flux_x[0]
                    for j in range(1, 4):
                        slope = slope + jnp.float32(table[i, j]) * flux_x[j]
                    flux_y = wind_y[s][r] * field[s][r]
                    for k in range(-3, 4):
                        slope = slope + coefficient[k] * rot(flux_y, -k)
                    moved = field[s][r] - slope
                    limited = jnp.minimum(jnp.maximum(moved, lower[s][e]), upper[s][e])
                    weighted[s][r] = mass[s][r] * limited
        summed = shared(weighted)
        fresh = [[None] * 8, [None] * 8]
        for s in range(2):
            for r in rows:
                value = jnp.float32(share_new) * (summed[s][r] * inverse[s][r])
                if share_start:
                    value = jnp.float32(share_start) * start[s][r] + value
                fresh[s][r] = value
        field = fresh
    for r in rows:
        out_ref[:, 0, r, :] = field[0][r]
        out_ref[:, 1, r, :] = field[0][r]


def remap_kernel(remap_ref, x_ref, out_ref):
    base = lax.axis_index("lev") * 8
    weight = [[remap_ref[a : a + 1, b : b + 1] for b in range(2)] for a in range(2)]
    for t in range(4):
        low, high = x_ref[base + 2 * t], x_ref[base + 2 * t + 1]
        for a in range(2):
            out_ref[a, t] = weight[a][0] * low + weight[a][1] * high


def vmem(count):
    return [pl.BlockSpec(memory_space=pltpu.VMEM)] * count


def step(tracer, node_mass, wind_x, wind_y, remap):
    count = lax.axis_size("py")
    whole = (8, 1, 8, LANES)
    packed = jnp.concatenate(
        [tracer.reshape(whole)]
        + [jnp.broadcast_to(part[None], whole) for part in (node_mass, wind_x, wind_y)],
        axis=1,
    )
    rows = lax.all_to_all(packed, "px", 0, 0, tiled=True)
    edge = jax.ShapeDtypeStruct((8, 8, LANES), jnp.float32)
    inside, cross = pl.pallas_call(
        edges_kernel,
        out_shape=(edge, edge),
        in_specs=vmem(1),
        out_specs=tuple(vmem(2)),
        compiler_params=PARAMS,
        name="edges",
    )(rows)
    cross_pairs = [(i, i + 1 if i % 2 else i - 1) for i in range(1, count - 1)]
    inside_pairs = [(i, i ^ 1) for i in range(count)]
    cross = lax.ppermute(cross, "py", cross_pairs)
    inside = lax.ppermute(inside, "py", inside_pairs)
    done = pl.pallas_call(
        sections_kernel,
        out_shape=jax.ShapeDtypeStruct((8, 2, 8, LANES), jnp.float32),
        in_specs=vmem(3),
        out_specs=vmem(1)[0],
        compiler_params=PARAMS,
        name="sections",
    )(rows, inside, cross)
    back = lax.all_to_all(done.reshape(16, 8, LANES), ("px", "lev"), 0, 0, tiled=True)
    return pl.pallas_call(
        remap_kernel,
        out_shape=jax.ShapeDtypeStruct((2, 4, 8, LANES), jnp.float32),
        in_specs=vmem(2),
        out_specs=vmem(1)[0],
        compiler_params=PARAMS,
        name="remap",
    )(remap, back)


def solution(mesh):
    in_specs = (
        P("lev", None, "px", "py"),
        P("lev", "px", "py"),
        P("lev", "px", "py"),
        P("lev", "px", "py"),
        P(),
    )
    out_specs = P(None, "lev", "px", "py")
    return jax.shard_map(
        step, mesh=mesh, in_specs=in_specs, out_specs=out_specs, check_vma=False
    )
```

```python
import jax
import jax.numpy as jnp
import numpy as np
from jax import lax
from jax.experimental import pallas as pl
from jax.experimental.pallas import tpu as pltpu
from jax.sharding import PartitionSpec as P


GLL_NODES = 4
LANES = 128
PARAMS = pltpu.CompilerParams(vmem_limit_bytes=8 * 1024 * 1024)
SLOT = 32

sentinel = 1e30
step_size = 0.1
section_weights = ((0.0, 1.0), (0.75, 0.25), (1.0 / 3.0, 2.0 / 3.0))


def derivative_table():
    points = np.array([-1.0, -(5.0 ** (-0.5)), 5.0 ** (-0.5), 1.0])
    number = points.shape[0]
    barycentric = np.array(
        [
            1.0
            / np.prod([points[outer] - points[inner] for inner in range(number) if inner != outer])
            for outer in range(number)
        ]
    )
    table = np.zeros((number, number))
    for outer in range(number):
        for inner in range(number):
            if inner != outer:
                table[outer, inner] = (
                    barycentric[inner] / barycentric[outer] / (points[outer] - points[inner])
                )
    for outer in range(number):
        table[outer, outer] = -np.sum(table[outer])
    return table


def rot(x, k):
    k = k % LANES
    return pltpu.roll(x, k, 1) if k else x


def lane_index():
    return lax.broadcasted_iota(jnp.int32, (8, LANES), 1)


def node_index():
    return lane_index() % GLL_NODES


def table_kernel(out_ref):
    table = derivative_table() * step_size
    node = node_index()
    for m in range(4):
        c = jnp.full((8, LANES), table[0, m], jnp.float32)
        for i in range(1, 4):
            c = jnp.where(node == i, jnp.float32(table[i, i ^ m]), c)
        out_ref[m] = c


def pack_kernel(first_ref, t_ref, m_ref, x_ref, y_ref, out_ref):
    common = [ref[0] for ref in (m_ref, x_ref, y_ref)]
    for i in range(8):
        out_ref[i, 0] = t_ref[0, i]
        for a in range(3):
            out_ref[i, a + 1] = common[a]


def gathered(r_ref, a, r):
    return r_ref[pl.ds(a * 8 + r, 8, stride=32), :]


def edges_kernel(r_ref, in_ref, cross_ref):
    slot = lane_index() // SLOT
    even = lax.axis_index("py") % 2 == 0
    for r in range(8):
        left = right = None
        for a in range(4):
            x = gathered(r_ref, a, r)
            lo, hi = rot(x, SLOT * a), rot(x, SLOT * a + SLOT)
            left = lo if a == 0 else jnp.where(slot == a, lo, left)
            right = hi if a == 0 else jnp.where(slot == a, hi, right)
        in_ref[r] = jnp.where(even, right, left)
        cross_ref[r] = jnp.where(even, left, right)


def sections_kernel(r_ref, in_ref, cross_ref, table_ref, out_ref):
    lane = lane_index()
    node = node_index()
    py = lax.axis_index("py")
    even = py % 2 == 0
    has_left = py > 0
    has_right = py < lax.axis_size("py") - 1
    exists = ((lane < 64) & has_right) | ((lane >= 64) & has_left)
    rim_node = (node == 0) | (node == 3)
    rim_lane = (lane == 0) | (lane == LANES - 1)
    partner = jnp.where(node == 0, lane - 1, jnp.where(node == 3, lane + 1, lane))
    partner = (partner + LANES) % LANES
    table = derivative_table() * step_size
    rows = range(8)

    def permuted(x, index):
        return jnp.take_along_axis(x, index, axis=1, mode="promise_in_bounds")

    def pairs(a, fill):
        own, halo = [], []
        for r in rows:
            from_right = jnp.where(even, in_ref[r], cross_ref[r])
            from_left = jnp.where(even, cross_ref[r], in_ref[r])
            second = jnp.where(
                lane >= LANES - SLOT, rot(from_left, -SLOT * a - SLOT), jnp.float32(fill)
            )
            second = jnp.where(lane < SLOT, rot(from_right, -SLOT * a), second)
            own.append(gathered(r_ref, a, r))
            halo.append(second)
        return [own, halo]

    def before(f, k):
        o, h = rot(f[0], k), rot(f[1], k)
        return jnp.where(lane < k, h, o), jnp.where(lane < k, o, h)

    def after(f, k):
        o, h = rot(f[0], -k), rot(f[1], -k)
        return jnp.where(lane >= LANES - k, h, o), jnp.where(lane >= LANES - k, o, h)

    def up(x):
        return pltpu.roll(x, 1, 0)

    def down(x):
        return pltpu.roll(x, 7, 0)

    def shared(f):
        f = [list(part) for part in f]
        for part in f:
            first, last = part[0], part[7]
            part[0] = first + up(last)
            part[7] = last + down(first)
            part[3] = part[4] = part[3] + part[4]
        for r in rows:
            own, halo = f[0][r], f[1][r]
            o, h = permuted(own, partner), permuted(halo, partner)
            f[0][r] = own + jnp.where(rim_node, jnp.where(rim_lane, h, o), 0.0)
            f[1][r] = halo + jnp.where(rim_node, jnp.where(rim_lane, o, h), 0.0)
        return f

    def extreme(f, op, missing):
        parts = []
        for s in range(2):
            halves = []
            for e in range(2):
                x = op(op(f[s][4 * e], f[s][4 * e + 1]), op(f[s][4 * e + 2], f[s][4 * e + 3]))
                x = op(x, permuted(x, lane ^ 1))
                x = op(x, permuted(x, lane ^ 2))
                if s == 1:
                    x = jnp.where(exists, x, missing)
                halves.append(x)
            zero, one = halves
            both = op(zero, one)
            parts.append((op(both, up(one)), op(both, down(zero))))
        result = [[None, None], [None, None]]
        for e in range(2):
            both = (parts[0][e], parts[1][e])
            lo, hi = before(both, 4), after(both, 4)
            for s in range(2):
                result[s][e] = op(op(both[s], lo[s]), hi[s])
        return result

    def slopes_x(f):
        outer, inner = f[0] - f[3], f[1] - f[2]
        even_part = (f[0] + f[3]) - (f[1] + f[2])
        result = [None] * 4
        for i in range(2):
            p = jnp.float32((table[i, 0] - table[i, 3]) / 2) * outer
            p = p + jnp.float32((table[i, 1] - table[i, 2]) / 2) * inner
            q = jnp.float32((table[i, 0] + table[i, 3]) / 2) * even_part
            result[i], result[3 - i] = p + q, p - q
        return result

    start = pairs(0, 0.0)
    mass = pairs(1, 1.0)
    wind_x = pairs(2, 0.0)
    wind_y = pairs(3, 0.0)
    coefficient = [table_ref[m] for m in range(4)]
    mass_sum = shared(mass)
    inverse = [
        [1.0 / m for m in mass_sum[0]],
        [jnp.where(exists, 1.0 / jnp.where(exists, m, 1.0), 0.0) for m in mass_sum[1]],
    ]
    field = start
    for share_start, share_new in section_weights:
        lower = extreme(field, jnp.minimum, sentinel)
        upper = extreme(field, jnp.maximum, -sentinel)
        weighted = [[None] * 8, [None] * 8]
        for s in range(2):
            for e in range(2):
                along_x = slopes_x([wind_x[s][4 * e + i] * field[s][4 * e + i] for i in range(4)])
                for i in range(4):
                    r = 4 * e + i
                    flux_y = wind_y[s][r] * field[s][r]
                    slope = along_x[i] + coefficient[0] * flux_y
                    for m in range(1, 4):
                        slope = slope + coefficient[m] * permuted(flux_y, lane ^ m)
                    moved = field[s][r] - slope
                    limited = jnp.minimum(jnp.maximum(moved, lower[s][e]), upper[s][e])
                    weighted[s][r] = mass[s][r] * limited
        summed = shared(weighted)
        fresh = [[None] * 8, [None] * 8]
        for s in range(2):
            for r in rows:
                value = summed[s][r] * inverse[s][r]
                if share_new != 1.0:
                    value = jnp.float32(share_new) * value
                if share_start:
                    value = jnp.float32(share_start) * start[s][r] + value
                fresh[s][r] = value
        field = fresh
    for r in rows:
        for m in range(2):
            out_ref[pl.ds(m * 8 + r, 8, stride=16), :] = field[0][r]


def remap_kernel(remap_ref, x_ref, out_ref):
    base = lax.axis_index("lev") * 8
    weight = [[remap_ref[a : a + 1, b : b + 1] for b in range(2)] for a in range(2)]
    for t in range(4):
        low, high = x_ref[base + 2 * t], x_ref[base + 2 * t + 1]
        for a in range(2):
            out_ref[a, t] = weight[a][0] * low + weight[a][1] * high


def vmem(count):
    return [pl.BlockSpec(memory_space=pltpu.VMEM)] * count


def step(tracer, node_mass, wind_x, wind_y, remap):
    count = lax.axis_size("py")
    tables = pl.pallas_call(
        table_kernel,
        out_shape=jax.ShapeDtypeStruct((4, 8, LANES), jnp.float32),
        out_specs=vmem(1)[0],
        compiler_params=PARAMS,
        cost_estimate=pl.CostEstimate(flops=10**10, bytes_accessed=10**7, transcendentals=0),
        name="tables",
    )()
    packed = pl.pallas_call(
        pack_kernel,
        out_shape=jax.ShapeDtypeStruct((8, 4, 8, LANES), jnp.float32),
        in_specs=vmem(5),
        out_specs=vmem(1)[0],
        compiler_params=PARAMS,
        name="pack",
    )(tables, tracer, node_mass, wind_x, wind_y)
    rows = lax.all_to_all(packed, "px", 0, 0, tiled=True).reshape(256, LANES)
    edge = jax.ShapeDtypeStruct((8, 8, LANES), jnp.float32)
    inside, cross = pl.pallas_call(
        edges_kernel,
        out_shape=(edge, edge),
        in_specs=vmem(1),
        out_specs=tuple(vmem(2)),
        compiler_params=PARAMS,
        name="edges",
    )(rows)
    cross_pairs = [(i, i + 1 if i % 2 else i - 1) for i in range(1, count - 1)]
    inside_pairs = [(i, i ^ 1) for i in range(count)]
    cross = lax.ppermute(cross, "py", cross_pairs)
    inside = lax.ppermute(inside, "py", inside_pairs)
    done = pl.pallas_call(
        sections_kernel,
        out_shape=jax.ShapeDtypeStruct((128, LANES), jnp.float32),
        in_specs=vmem(4),
        out_specs=vmem(1)[0],
        compiler_params=PARAMS,
        name="sections",
    )(rows, inside, cross, tables)
    back = lax.all_to_all(done.reshape(16, 8, LANES), ("px", "lev"), 0, 0, tiled=True)
    return pl.pallas_call(
        remap_kernel,
        out_shape=jax.ShapeDtypeStruct((2, 4, 8, LANES), jnp.float32),
        in_specs=vmem(2),
        out_specs=vmem(1)[0],
        compiler_params=PARAMS,
        name="remap",
    )(remap, back)


def solution(mesh):
    in_specs = (
        P("lev", None, "px", "py"),
        P("lev", "px", "py"),
        P("lev", "px", "py"),
        P("lev", "px", "py"),
        P(),
    )
    out_specs = P(None, "lev", "px", "py")
    return jax.shard_map(step, mesh=mesh, in_specs=in_specs, out_specs=out_specs, check_vma=False)
```

```python
import functools

import jax
import jax.numpy as jnp
import numpy as np
from jax import lax
from jax.experimental import pallas as pl
from jax.experimental.pallas import tpu as pltpu
from jax.sharding import PartitionSpec as P

GLL_NODES = 4
LANES = 128
PARAMS = pltpu.CompilerParams(vmem_limit_bytes=8 * 1024 * 1024)
SLOT = 32
WINDOW = 96
HALO = 24

sentinel = 1e30
step_size = 0.1
section_weights = ((0.0, 1.0), (0.75, 0.25), (1.0 / 3.0, 2.0 / 3.0))


def derivative_table():
    points = np.array([-1.0, -(5.0 ** (-0.5)), 5.0 ** (-0.5), 1.0])
    number = points.shape[0]
    barycentric = np.array(
        [
            1.0
            / np.prod([points[outer] - points[inner] for inner in range(number) if inner != outer])
            for outer in range(number)
        ]
    )
    table = np.zeros((number, number))
    for outer in range(number):
        for inner in range(number):
            if inner != outer:
                table[outer, inner] = (
                    barycentric[inner] / barycentric[outer] / (points[outer] - points[inner])
                )
    for outer in range(number):
        table[outer, outer] = -np.sum(table[outer])
    return table


def rot(x, k):
    k = k % LANES
    return pltpu.roll(x, k, 1) if k else x


def lane_index():
    return lax.broadcasted_iota(jnp.int32, (8, LANES), 1)


def node_index():
    return lane_index() % GLL_NODES


def table_kernel(out_ref):
    table = derivative_table() * step_size
    node = node_index()
    for m in range(4):
        c = jnp.full((8, LANES), table[0, m], jnp.float32)
        for i in range(1, 4):
            c = jnp.where(node == i, jnp.float32(table[i, i ^ m]), c)
        out_ref[m] = c


def pack_kernel(first_ref, t_ref, m_ref, x_ref, y_ref, out_ref):
    window = lane_index() < WINDOW
    for half in range(2):
        shift = -SLOT * half
        piece = [rot(y_ref[0], WINDOW - SLOT * u + shift) for u in range(3)]
        mass = jnp.where(window, rot(m_ref[0], shift), piece[2])
        wind = rot(x_ref[0], shift)
        for q in range(4):
            for u in range(2):
                t = rot(t_ref[0, 2 * q + u], shift)
                out_ref[2 * q + half, u] = jnp.where(window, t, piece[u])
            out_ref[2 * q + half, 2] = mass
            out_ref[2 * q + half, 3] = wind


def gathered(r_ref, u, r):
    return r_ref[pl.ds(u * 8 + r, 8, stride=32), :]


def moved_lanes(x, left, if_left, if_right):
    return pltpu.roll(x, jnp.where(left, if_left % LANES, if_right % LANES), 1)


def edge_kernel(r_ref, out_ref):
    slot = lane_index() // HALO
    left = lax.axis_index("px") % 2 == 0
    for r in range(8):
        unit = [gathered(r_ref, u, r) for u in range(4)]
        edge = moved_lanes(jnp.where(left, unit[0], unit[2]), left, 0, -8)
        for a in range(4):
            piece = moved_lanes(unit[a], left, HALO * a, HALO * a + HALO - WINDOW)
            edge = jnp.where(slot == a, piece, edge)
        out_ref[r] = edge


def sections_kernel(r_ref, halo_ref, table_ref, out_ref):
    lane = lane_index()
    node = node_index()
    py = lax.axis_index("py")
    left = lax.axis_index("px") % 2 == 0
    has_halo = (left & (py > 0)) | (~left & (py < lax.axis_size("py") - 1))
    exists = (lane < WINDOW) | has_halo
    inner_end = jnp.where(left, LANES, WINDOW + HALO)
    in_halo = (lane >= inner_end - HALO) & (lane < inner_end)
    rim_node = (node == 0) | (node == 3)
    partner = jnp.where(node == 0, lane - 1, jnp.where(node == 3, lane + 1, lane))
    partner = (partner + LANES) % LANES
    table = derivative_table() * step_size
    rows = range(8)

    def permuted(x, index):
        return jnp.take_along_axis(x, index, axis=1, mode="promise_in_bounds")

    def completed(a, fill):
        result = []
        for r in rows:
            if a < 4:
                x = gathered(r_ref, a, r)
            else:
                unit = [gathered(r_ref, u, r) for u in range(3)]
                x = jnp.where(lane < 2 * SLOT, rot(unit[1], 2 * SLOT), rot(unit[2], 3 * SLOT))
                x = jnp.where(lane < SLOT, rot(unit[0], SLOT), x)
            halo = moved_lanes(halo_ref[r], left, LANES - HALO - HALO * a, WINDOW - HALO * a)
            halo = jnp.where(in_halo, halo, jnp.float32(fill))
            result.append(jnp.where(lane < WINDOW, x, halo))
        return result

    def up(x):
        return pltpu.roll(x, 1, 0)

    def down(x):
        return pltpu.roll(x, 7, 0)

    def shared(f):
        f = list(f)
        first, last = f[0], f[7]
        f[0] = first + up(last)
        f[7] = last + down(first)
        f[3] = f[4] = f[3] + f[4]
        return [x + jnp.where(rim_node, permuted(x, partner), 0.0) for x in f]

    def extreme(f, op, missing):
        halves = []
        for e in range(2):
            x = op(op(f[4 * e], f[4 * e + 1]), op(f[4 * e + 2], f[4 * e + 3]))
            x = op(x, permuted(x, lane ^ 1))
            x = op(x, permuted(x, lane ^ 2))
            x = jnp.where(exists, x, missing)
            halves.append(op(op(x, rot(x, 4)), rot(x, -4)))
        zero, one = halves
        both = op(zero, one)
        return op(both, up(one)), op(both, down(zero))

    def slopes_x(f):
        outer, inner = f[0] - f[3], f[1] - f[2]
        even_part = (f[0] + f[3]) - (f[1] + f[2])
        result = [None] * 4
        for i in range(2):
            p = jnp.float32((table[i, 0] - table[i, 3]) / 2) * outer
            p = p + jnp.float32((table[i, 1] - table[i, 2]) / 2) * inner
            q = jnp.float32((table[i, 0] + table[i, 3]) / 2) * even_part
            result[i], result[3 - i] = p + q, p - q
        return result

    mass = completed(2, 1.0)
    wind_x = completed(3, 0.0)
    wind_y = completed(4, 0.0)
    coefficient = [table_ref[m] for m in range(4)]
    inverse = [jnp.where(exists, 1.0 / jnp.where(exists, m, 1.0), 0.0) for m in shared(mass)]
    finished = []
    for tracer in range(2):
        start = completed(tracer, 0.0)
        field = start
        for share_start, share_new in section_weights:
            lower = extreme(field, jnp.minimum, sentinel)
            upper = extreme(field, jnp.maximum, -sentinel)
            weighted = [None] * 8
            for e in range(2):
                along_x = slopes_x([wind_x[4 * e + i] * field[4 * e + i] for i in range(4)])
                for i in range(4):
                    r = 4 * e + i
                    flux_y = wind_y[r] * field[r]
                    slope = along_x[i] + coefficient[0] * flux_y
                    for m in range(1, 4):
                        slope = slope + coefficient[m] * permuted(flux_y, lane ^ m)
                    limited = jnp.minimum(jnp.maximum(field[r] - slope, lower[e]), upper[e])
                    weighted[r] = mass[r] * limited
            summed = shared(weighted)
            fresh = [None] * 8
            for r in rows:
                value = summed[r] * inverse[r]
                if share_new != 1.0:
                    value = jnp.float32(share_new) * value
                if share_start:
                    value = jnp.float32(share_start) * start[r] + value
                fresh[r] = value
            field = fresh
        finished.append(field)
    for r in rows:
        low = moved_lanes(finished[0][r], left, 0, -SLOT)
        high = moved_lanes(finished[1][r], left, 2 * SLOT, SLOT)
        both = jnp.where(lane < 2 * SLOT, low, high)
        for m in range(2):
            out_ref[pl.ds(m * 8 + r, 8, stride=16), :] = both


def remap_kernel(remap_ref, x_ref, out_ref):
    base = lax.axis_index("lev") * 8
    low = lane_index() < LANES // 2
    weight = [[remap_ref[a : a + 1, b : b + 1] for b in range(2)] for a in range(2)]
    for q in range(2):
        first, second = [], []
        for level in range(2):
            left = x_ref[base + 4 * q + level]
            right = x_ref[base + 4 * q + 2 + level]
            first.append(jnp.where(low, left, rot(right, LANES // 2)))
            second.append(jnp.where(low, rot(left, LANES // 2), right))
        for a in range(2):
            out_ref[a, 2 * q] = weight[a][0] * first[0] + weight[a][1] * first[1]
            out_ref[a, 2 * q + 1] = weight[a][0] * second[0] + weight[a][1] * second[1]


def vmem(count):
    return [pl.BlockSpec(memory_space=pltpu.VMEM)] * count


def shards(tracer, node_mass, wind_x, wind_y, remap):
    count = lax.axis_size("py")
    tables = pl.pallas_call(
        table_kernel,
        out_shape=jax.ShapeDtypeStruct((4, 8, LANES), jnp.float32),
        out_specs=vmem(1)[0],
        compiler_params=PARAMS,
        cost_estimate=pl.CostEstimate(flops=10**10, bytes_accessed=10**7, transcendentals=0),
        name="tables",
    )()
    packed = pl.pallas_call(
        pack_kernel,
        out_shape=jax.ShapeDtypeStruct((8, 4, 8, LANES), jnp.float32),
        in_specs=vmem(5),
        out_specs=vmem(1)[0],
        compiler_params=PARAMS,
        name="pack",
    )(tables, tracer, node_mass, wind_x, wind_y)
    rows = lax.all_to_all(packed, "px", 0, 0, tiled=True).reshape(256, LANES)
    edge = pl.pallas_call(
        edge_kernel,
        out_shape=jax.ShapeDtypeStruct((8, 8, LANES), jnp.float32),
        in_specs=vmem(1),
        out_specs=vmem(1)[0],
        compiler_params=PARAMS,
        name="edge",
    )(rows)
    pairs = []
    for q in range(0, lax.axis_size("px"), 2):
        for py in range(1, count):
            a, b = q * count + py, (q + 1) * count + py - 1
            pairs += [(a, b), (b, a)]
    halo = lax.ppermute(edge, ("px", "py"), pairs)
    done = pl.pallas_call(
        sections_kernel,
        out_shape=jax.ShapeDtypeStruct((128, LANES), jnp.float32),
        in_specs=vmem(3),
        out_specs=vmem(1)[0],
        compiler_params=PARAMS,
        name="sections",
    )(rows, halo, tables)
    back = lax.all_to_all(done.reshape(16, 8, LANES), ("px", "lev"), 0, 0, tiled=True)
    return pl.pallas_call(
        remap_kernel,
        out_shape=jax.ShapeDtypeStruct((2, 4, 8, LANES), jnp.float32),
        in_specs=vmem(2),
        out_specs=vmem(1)[0],
        compiler_params=PARAMS,
        name="remap",
    )(remap, back)


def solution(mesh):
    in_specs = (
        P("lev", None, "px", "py"),
        P("lev", "px", "py"),
        P("lev", "px", "py"),
        P("lev", "px", "py"),
        P(),
    )
    out_specs = P(None, "lev", "px", "py")
    return jax.shard_map(shards, mesh=mesh, in_specs=in_specs, out_specs=out_specs, check_vma=False)
```

```python
import functools

import jax
import jax.numpy as jnp
import numpy as np
from jax import lax
from jax.experimental import pallas as pl
from jax.experimental.pallas import tpu as pltpu
from jax.sharding import PartitionSpec as P

GLL_NODES = 4
LANES = 128
PARAMS = pltpu.CompilerParams(vmem_limit_bytes=8 * 1024 * 1024)
SLOT = 32
WINDOW = 96
HALO = 24

sentinel = 1e30
step_size = 0.1
section_weights = ((0.0, 1.0), (0.75, 0.25), (1.0 / 3.0, 2.0 / 3.0))


def derivative_table():
    points = np.array([-1.0, -(5.0 ** (-0.5)), 5.0 ** (-0.5), 1.0])
    number = points.shape[0]
    barycentric = np.array(
        [
            1.0
            / np.prod([points[outer] - points[inner] for inner in range(number) if inner != outer])
            for outer in range(number)
        ]
    )
    table = np.zeros((number, number))
    for outer in range(number):
        for inner in range(number):
            if inner != outer:
                table[outer, inner] = (
                    barycentric[inner] / barycentric[outer] / (points[outer] - points[inner])
                )
    for outer in range(number):
        table[outer, outer] = -np.sum(table[outer])
    return table


def rot(x, k):
    k = k % LANES
    return pltpu.roll(x, k, 1) if k else x


def lane_index():
    return lax.broadcasted_iota(jnp.int32, (8, LANES), 1)


def node_index():
    return lane_index() % GLL_NODES


def table_kernel(out_ref):
    table = derivative_table() * step_size
    node = node_index()
    for m in range(4):
        c = jnp.full((8, LANES), table[0, m], jnp.float32)
        for i in range(1, 4):
            c = jnp.where(node == i, jnp.float32(table[i, i ^ m]), c)
        out_ref[m] = c


def pack_kernel(first_ref, t_ref, m_ref, x_ref, y_ref, out_ref):
    odd = lax.axis_index("py") % 2
    window = lane_index() < WINDOW
    for half in range(2):
        shift = -SLOT * half
        piece = [rot(y_ref[0], WINDOW - SLOT * u + shift) for u in range(3)]
        mass = jnp.where(window, rot(m_ref[0], shift), piece[2])
        wind = rot(x_ref[0], shift)
        place = jnp.where(odd == 1, 1 - half, half)
        for q in range(4):
            for u in range(2):
                t = rot(t_ref[0, 2 * q + u], shift)
                out_ref[2 * q + place, u] = jnp.where(window, t, piece[u])
            out_ref[2 * q + place, 2] = mass
            out_ref[2 * q + place, 3] = wind


def gathered(r_ref, u, r):
    return r_ref[pl.ds(u * 8 + r, 8, stride=32), :]


def works_left():
    return (lax.axis_index("px") + lax.axis_index("py")) % 2 == 0


def moved_lanes(x, left, if_left, if_right):
    return pltpu.roll(x, jnp.where(left, if_left % LANES, if_right % LANES), 1)


def edge_kernel(r_ref, out_ref):
    slot = lane_index() // HALO
    left = works_left()
    for r in range(8):
        unit = [gathered(r_ref, u, r) for u in range(4)]
        edge = moved_lanes(jnp.where(left, unit[0], unit[2]), left, 0, -8)
        for a in range(4):
            piece = moved_lanes(unit[a], left, HALO * a, HALO * a + HALO - WINDOW)
            edge = jnp.where(slot == a, piece, edge)
        out_ref[r] = edge


def collect_kernel(r_ref, out_ref):
    lane = lane_index()
    for r in range(8):
        unit = [gathered(r_ref, u, r) for u in range(4)]
        last = jnp.where(lane < 2 * SLOT, rot(unit[1], 2 * SLOT), rot(unit[2], 3 * SLOT))
        last = jnp.where(lane < SLOT, rot(unit[0], SLOT), last)
        for a in range(4):
            out_ref[a, r] = unit[a]
        out_ref[4, r] = last


def sections_kernel(own_ref, halo_ref, table_ref, out_ref):
    lane = lane_index()
    node = node_index()
    py = lax.axis_index("py")
    left = works_left()
    has_halo = (left & (py > 0)) | (~left & (py < lax.axis_size("py") - 1))
    exists = (lane < WINDOW) | has_halo
    inner_end = jnp.where(left, LANES, WINDOW + HALO)
    in_halo = (lane >= inner_end - HALO) & (lane < inner_end)
    rim_node = (node == 0) | (node == 3)
    partner = jnp.where(node == 0, lane - 1, jnp.where(node == 3, lane + 1, lane))
    partner = (partner + LANES) % LANES
    table = derivative_table() * step_size
    rows = range(8)

    def permuted(x, index):
        return jnp.take_along_axis(x, index, axis=1, mode="promise_in_bounds")

    def completed(a, fill):
        result = []
        for r in rows:
            halo = moved_lanes(halo_ref[r], left, LANES - HALO - HALO * a, WINDOW - HALO * a)
            halo = jnp.where(in_halo, halo, jnp.float32(fill))
            result.append(jnp.where(lane < WINDOW, own_ref[a, r], halo))
        return result

    def up(x):
        return pltpu.roll(x, 1, 0)

    def down(x):
        return pltpu.roll(x, 7, 0)

    def shared(f):
        f = list(f)
        first, last = f[0], f[7]
        f[0] = first + up(last)
        f[7] = last + down(first)
        f[3] = f[4] = f[3] + f[4]
        return [x + jnp.where(rim_node, permuted(x, partner), 0.0) for x in f]

    def extreme(f, op, missing):
        halves = []
        for e in range(2):
            x = op(op(f[4 * e], f[4 * e + 1]), op(f[4 * e + 2], f[4 * e + 3]))
            x = op(x, permuted(x, lane ^ 1))
            x = op(x, permuted(x, lane ^ 2))
            x = jnp.where(exists, x, missing)
            halves.append(op(op(x, rot(x, 4)), rot(x, -4)))
        zero, one = halves
        both = op(zero, one)
        return op(both, up(one)), op(both, down(zero))

    def slopes_x(f):
        outer, inner = f[0] - f[3], f[1] - f[2]
        even_part = (f[0] + f[3]) - (f[1] + f[2])
        result = [None] * 4
        for i in range(2):
            p = jnp.float32((table[i, 0] - table[i, 3]) / 2) * outer
            p = p + jnp.float32((table[i, 1] - table[i, 2]) / 2) * inner
            q = jnp.float32((table[i, 0] + table[i, 3]) / 2) * even_part
            result[i], result[3 - i] = p + q, p - q
        return result

    mass = completed(2, 1.0)
    wind_x = completed(3, 0.0)
    wind_y = completed(4, 0.0)
    coefficient = [table_ref[m] for m in range(4)]
    inverse = [jnp.where(exists, 1.0 / jnp.where(exists, m, 1.0), 0.0) for m in shared(mass)]
    finished = []
    for tracer in range(2):
        start = completed(tracer, 0.0)
        field = start
        for share_start, share_new in section_weights:
            lower = extreme(field, jnp.minimum, sentinel)
            upper = extreme(field, jnp.maximum, -sentinel)
            weighted = [None] * 8
            for e in range(2):
                along_x = slopes_x([wind_x[4 * e + i] * field[4 * e + i] for i in range(4)])
                for i in range(4):
                    r = 4 * e + i
                    flux_y = wind_y[r] * field[r]
                    slope = along_x[i] + coefficient[0] * flux_y
                    for m in range(1, 4):
                        slope = slope + coefficient[m] * permuted(flux_y, lane ^ m)
                    limited = jnp.minimum(jnp.maximum(field[r] - slope, lower[e]), upper[e])
                    weighted[r] = mass[r] * limited
            summed = shared(weighted)
            fresh = [None] * 8
            for r in rows:
                value = summed[r] * inverse[r]
                if share_new != 1.0:
                    value = jnp.float32(share_new) * value
                if share_start:
                    value = jnp.float32(share_start) * start[r] + value
                fresh[r] = value
            field = fresh
        finished.append(field)
    for r in rows:
        low = moved_lanes(finished[0][r], left, 0, -SLOT)
        high = moved_lanes(finished[1][r], left, 2 * SLOT, SLOT)
        both = jnp.where(lane < 2 * SLOT, low, high)
        for m in range(2):
            out_ref[pl.ds(m * 64 + r, 8, stride=8), :] = both


def remap_kernel(remap_ref, x_ref, out_ref):
    base = lax.axis_index("lev") * 4
    odd = lax.axis_index("py") % 2
    low = lane_index() < LANES // 2
    weight = [[remap_ref[a : a + 1, b : b + 1] for b in range(2)] for a in range(2)]
    for q in range(2):
        first, second = [], []
        for level in range(2):
            left = x_ref[base + 2 * q + odd + 8 * level]
            right = x_ref[base + 2 * q + 1 - odd + 8 * level]
            first.append(jnp.where(low, left, rot(right, LANES // 2)))
            second.append(jnp.where(low, rot(left, LANES // 2), right))
        for a in range(2):
            out_ref[a, 2 * q] = weight[a][0] * first[0] + weight[a][1] * first[1]
            out_ref[a, 2 * q + 1] = weight[a][0] * second[0] + weight[a][1] * second[1]


def vmem(count):
    return [pl.BlockSpec(memory_space=pltpu.VMEM)] * count


def shards(tracer, node_mass, wind_x, wind_y, remap):
    count = lax.axis_size("py")
    tables = pl.pallas_call(
        table_kernel,
        out_shape=jax.ShapeDtypeStruct((4, 8, LANES), jnp.float32),
        out_specs=vmem(1)[0],
        compiler_params=PARAMS,
        cost_estimate=pl.CostEstimate(flops=10**10, bytes_accessed=10**7, transcendentals=0),
        name="tables",
    )()
    packed = pl.pallas_call(
        pack_kernel,
        out_shape=jax.ShapeDtypeStruct((8, 4, 8, LANES), jnp.float32),
        in_specs=vmem(5),
        out_specs=vmem(1)[0],
        compiler_params=PARAMS,
        name="pack",
    )(tables, tracer, node_mass, wind_x, wind_y)
    rows = lax.all_to_all(packed, "px", 0, 0, tiled=True).reshape(256, LANES)
    edge = pl.pallas_call(
        edge_kernel,
        out_shape=jax.ShapeDtypeStruct((8, 8, LANES), jnp.float32),
        in_specs=vmem(1),
        out_specs=vmem(1)[0],
        compiler_params=PARAMS,
        name="edge",
    )(rows)
    pairs = []
    for px in range(lax.axis_size("px")):
        for py in range(2 - px % 2, count, 2):
            a = px * count + py
            pairs += [(a, a - 1), (a - 1, a)]
    halo = lax.ppermute(edge, ("px", "py"), pairs)
    own = pl.pallas_call(
        collect_kernel,
        out_shape=jax.ShapeDtypeStruct((5, 8, 8, LANES), jnp.float32),
        in_specs=vmem(1),
        out_specs=vmem(1)[0],
        compiler_params=PARAMS,
        cost_estimate=pl.CostEstimate(flops=10**5, bytes_accessed=300000, transcendentals=0),
        name="collect",
    )(rows)
    done = pl.pallas_call(
        sections_kernel,
        out_shape=jax.ShapeDtypeStruct((128, LANES), jnp.float32),
        in_specs=vmem(3),
        out_specs=vmem(1)[0],
        compiler_params=PARAMS,
        name="sections",
    )(own, halo, tables)
    back = lax.all_to_all(done.reshape(16, 8, LANES), ("lev", "px"), 0, 0, tiled=True)
    return pl.pallas_call(
        remap_kernel,
        out_shape=jax.ShapeDtypeStruct((2, 4, 8, LANES), jnp.float32),
        in_specs=vmem(2),
        out_specs=vmem(1)[0],
        compiler_params=PARAMS,
        name="remap",
    )(remap, back)


def solution(mesh):
    in_specs = (
        P("lev", None, "px", "py"),
        P("lev", "px", "py"),
        P("lev", "px", "py"),
        P("lev", "px", "py"),
        P(),
    )
    out_specs = P(None, "lev", "px", "py")
    return jax.shard_map(shards, mesh=mesh, in_specs=in_specs, out_specs=out_specs, check_vma=False)
```

```python
import functools

import jax
import jax.numpy as jnp
import numpy as np
from jax import lax
from jax.experimental import pallas as pl
from jax.experimental.pallas import tpu as pltpu
from jax.sharding import PartitionSpec as P

GLL_NODES = 4
LANES = 128
PARAMS = pltpu.CompilerParams(vmem_limit_bytes=8 * 1024 * 1024)
SLOT = 32
WINDOW = 96
HALO = 24

sentinel = 1e30
step_size = 0.1
section_weights = ((0.0, 1.0), (0.75, 0.25), (1.0 / 3.0, 2.0 / 3.0))


def derivative_table():
    points = np.array([-1.0, -(5.0 ** (-0.5)), 5.0 ** (-0.5), 1.0])
    number = points.shape[0]
    barycentric = np.array(
        [
            1.0
            / np.prod([points[outer] - points[inner] for inner in range(number) if inner != outer])
            for outer in range(number)
        ]
    )
    table = np.zeros((number, number))
    for outer in range(number):
        for inner in range(number):
            if inner != outer:
                table[outer, inner] = (
                    barycentric[inner] / barycentric[outer] / (points[outer] - points[inner])
                )
    for outer in range(number):
        table[outer, outer] = -np.sum(table[outer])
    return table


def rot(x, k):
    k = k % LANES
    return pltpu.roll(x, k, 1) if k else x


def lane_index():
    return lax.broadcasted_iota(jnp.int32, (8, LANES), 1)


def node_index():
    return lane_index() % GLL_NODES


def table_kernel(out_ref):
    table = derivative_table() * step_size
    source = lax.broadcasted_iota(jnp.int32, (LANES, LANES), 0)
    target = lax.broadcasted_iota(jnp.int32, (LANES, LANES), 1)
    place = (target % GLL_NODES) * GLL_NODES + source % GLL_NODES
    c = jnp.zeros((LANES, LANES), jnp.float32)
    for i in range(GLL_NODES):
        for j in range(GLL_NODES):
            c = jnp.where(place == i * GLL_NODES + j, jnp.float32(table[i, j]), c)
    c = jnp.where(source // GLL_NODES == target // GLL_NODES, c, 0.0)
    high = c.astype(jnp.bfloat16)
    out_ref[0] = high
    out_ref[1] = (c - high.astype(jnp.float32)).astype(jnp.bfloat16)


def pack_kernel(first_ref, t_ref, m_ref, x_ref, y_ref, out_ref):
    odd = lax.axis_index("py") % 2
    window = lane_index() < WINDOW
    for half in range(2):
        shift = -SLOT * half
        piece = [rot(y_ref[0], WINDOW - SLOT * u + shift) for u in range(3)]
        mass = jnp.where(window, rot(m_ref[0], shift), piece[2])
        wind = rot(x_ref[0], shift)
        place = jnp.where(odd == 1, 1 - half, half)
        for q in range(4):
            for u in range(2):
                t = rot(t_ref[0, 2 * q + u], shift)
                out_ref[2 * q + place, u] = jnp.where(window, t, piece[u])
            out_ref[2 * q + place, 2] = mass
            out_ref[2 * q + place, 3] = wind


def gathered(r_ref, u, r):
    return r_ref[pl.ds(u * 8 + r, 8, stride=32), :]


def works_left():
    return (lax.axis_index("px") + lax.axis_index("py")) % 2 == 0


def moved_lanes(x, left, if_left, if_right):
    return pltpu.roll(x, jnp.where(left, if_left % LANES, if_right % LANES), 1)


def edge_kernel(r_ref, out_ref):
    slot = lane_index() // HALO
    left = works_left()
    for r in range(8):
        unit = [gathered(r_ref, u, r) for u in range(4)]
        edge = moved_lanes(jnp.where(left, unit[0], unit[2]), left, 0, -8)
        for a in range(4):
            piece = moved_lanes(unit[a], left, HALO * a, HALO * a + HALO - WINDOW)
            edge = jnp.where(slot == a, piece, edge)
        out_ref[r] = edge


def collect_kernel(r_ref, out_ref):
    lane = lane_index()
    for r in range(8):
        unit = [gathered(r_ref, u, r) for u in range(4)]
        last = jnp.where(lane < 2 * SLOT, rot(unit[1], 2 * SLOT), rot(unit[2], 3 * SLOT))
        last = jnp.where(lane < SLOT, rot(unit[0], SLOT), last)
        for a in range(4):
            out_ref[a, r] = unit[a]
        out_ref[4, r] = last


def sections_kernel(own_ref, halo_ref, table_ref, out_ref):
    lane = lane_index()
    node = node_index()
    py = lax.axis_index("py")
    left = works_left()
    has_halo = (left & (py > 0)) | (~left & (py < lax.axis_size("py") - 1))
    exists = (lane < WINDOW) | has_halo
    inner_end = jnp.where(left, LANES, WINDOW + HALO)
    in_halo = (lane >= inner_end - HALO) & (lane < inner_end)
    rim_node = (node == 0) | (node == 3)
    partner = jnp.where(node == 0, lane - 1, jnp.where(node == 3, lane + 1, lane))
    partner = (partner + LANES) % LANES
    table = derivative_table() * step_size
    rows = range(8)

    def permuted(x, index):
        return jnp.take_along_axis(x, index, axis=1, mode="promise_in_bounds")

    def completed(a, fill):
        result = []
        for r in rows:
            halo = moved_lanes(halo_ref[r], left, LANES - HALO - HALO * a, WINDOW - HALO * a)
            halo = jnp.where(in_halo, halo, jnp.float32(fill))
            result.append(jnp.where(lane < WINDOW, own_ref[a, r], halo))
        return result

    def up(x):
        return pltpu.roll(x, 1, 0)

    def down(x):
        return pltpu.roll(x, 7, 0)

    def shared(f):
        f = list(f)
        first, last = f[0], f[7]
        f[0] = first + up(last)
        f[7] = last + down(first)
        f[3] = f[4] = f[3] + f[4]
        return [x + jnp.where(rim_node, permuted(x, partner), 0.0) for x in f]

    def extreme(f, op, missing):
        halves = []
        for e in range(2):
            x = op(op(f[4 * e], f[4 * e + 1]), op(f[4 * e + 2], f[4 * e + 3]))
            x = op(x, permuted(x, lane ^ 1))
            x = op(x, permuted(x, lane ^ 2))
            x = jnp.where(exists, x, missing)
            halves.append(op(op(x, rot(x, 4)), rot(x, -4)))
        zero, one = halves
        both = op(zero, one)
        return op(both, up(one)), op(both, down(zero))

    def slopes_x(f):
        outer, inner = f[0] - f[3], f[1] - f[2]
        even_part = (f[0] + f[3]) - (f[1] + f[2])
        result = [None] * 4
        for i in range(2):
            p = jnp.float32((table[i, 0] - table[i, 3]) / 2) * outer
            p = p + jnp.float32((table[i, 1] - table[i, 2]) / 2) * inner
            q = jnp.float32((table[i, 0] + table[i, 3]) / 2) * even_part
            result[i], result[3 - i] = p + q, p - q
        return result

    mass = completed(2, 1.0)
    wind_x = completed(3, 0.0)
    wind_y = completed(4, 0.0)
    inverse = [jnp.where(exists, 1.0 / jnp.where(exists, m, 1.0), 0.0) for m in shared(mass)]
    starts = [completed(tracer, 0.0) for tracer in range(2)]
    fields = list(starts)
    for share_start, share_new in section_weights:
        flux = jnp.concatenate([wind_y[r] * f[r] for f in fields for r in rows], axis=0)
        high = flux.astype(jnp.bfloat16)
        low = (flux - high.astype(jnp.float32)).astype(jnp.bfloat16)
        both = jnp.concatenate([high, low], axis=0)
        product = jnp.dot(both, table_ref[0], preferred_element_type=jnp.float32)
        small = jnp.dot(high, table_ref[1], preferred_element_type=jnp.float32)
        along_y = (product[128:] + small) + product[:128]
        lowers = [extreme(f, jnp.minimum, sentinel) for f in fields]
        uppers = [extreme(f, jnp.maximum, -sentinel) for f in fields]
        weighted = [[None] * 8, [None] * 8]
        for e in range(2):
            for t in range(2):
                field = fields[t]
                along_x = slopes_x([wind_x[4 * e + i] * field[4 * e + i] for i in range(4)])
                for i in range(4):
                    r = 4 * e + i
                    at = 64 * t + 8 * r
                    moved = field[r] - (along_x[i] + along_y[at : at + 8])
                    limited = jnp.minimum(jnp.maximum(moved, lowers[t][e]), uppers[t][e])
                    weighted[t][r] = mass[r] * limited
        summed = [shared(w) for w in weighted]
        fresh = [[None] * 8, [None] * 8]
        for r in rows:
            for t in range(2):
                value = summed[t][r] * inverse[r]
                if share_new != 1.0:
                    value = jnp.float32(share_new) * value
                if share_start:
                    value = jnp.float32(share_start) * starts[t][r] + value
                fresh[t][r] = value
        fields = fresh
    finished = fields
    for r in rows:
        low = moved_lanes(finished[0][r], left, 0, -SLOT)
        high = moved_lanes(finished[1][r], left, 2 * SLOT, SLOT)
        both = jnp.where(lane < 2 * SLOT, low, high)
        for m in range(2):
            out_ref[pl.ds(m * 64 + r, 8, stride=8), :] = both


def remap_kernel(remap_ref, x_ref, out_ref):
    base = lax.axis_index("lev") * 4
    odd = lax.axis_index("py") % 2
    low = lane_index() < LANES // 2
    weight = [[remap_ref[a : a + 1, b : b + 1] for b in range(2)] for a in range(2)]
    for q in range(2):
        first, second = [], []
        for level in range(2):
            left = x_ref[base + 2 * q + odd + 8 * level]
            right = x_ref[base + 2 * q + 1 - odd + 8 * level]
            first.append(jnp.where(low, left, rot(right, LANES // 2)))
            second.append(jnp.where(low, rot(left, LANES // 2), right))
        for a in range(2):
            out_ref[a, 2 * q] = weight[a][0] * first[0] + weight[a][1] * first[1]
            out_ref[a, 2 * q + 1] = weight[a][0] * second[0] + weight[a][1] * second[1]


def vmem(count):
    return [pl.BlockSpec(memory_space=pltpu.VMEM)] * count


def shards(tracer, node_mass, wind_x, wind_y, remap):
    count = lax.axis_size("py")
    tables = pl.pallas_call(
        table_kernel,
        out_shape=jax.ShapeDtypeStruct((2, LANES, LANES), jnp.bfloat16),
        out_specs=vmem(1)[0],
        compiler_params=PARAMS,
        cost_estimate=pl.CostEstimate(flops=10**10, bytes_accessed=10**7, transcendentals=0),
        name="tables",
    )()
    packed = pl.pallas_call(
        pack_kernel,
        out_shape=jax.ShapeDtypeStruct((8, 4, 8, LANES), jnp.float32),
        in_specs=vmem(5),
        out_specs=vmem(1)[0],
        compiler_params=PARAMS,
        name="pack",
    )(tables, tracer, node_mass, wind_x, wind_y)
    rows = lax.all_to_all(packed, "px", 0, 0, tiled=True).reshape(256, LANES)
    edge = pl.pallas_call(
        edge_kernel,
        out_shape=jax.ShapeDtypeStruct((8, 8, LANES), jnp.float32),
        in_specs=vmem(1),
        out_specs=vmem(1)[0],
        compiler_params=PARAMS,
        name="edge",
    )(rows)
    pairs = []
    for px in range(lax.axis_size("px")):
        for py in range(2 - px % 2, count, 2):
            a = px * count + py
            pairs += [(a, a - 1), (a - 1, a)]
    halo = lax.ppermute(edge, ("px", "py"), pairs)
    own = pl.pallas_call(
        collect_kernel,
        out_shape=jax.ShapeDtypeStruct((5, 8, 8, LANES), jnp.float32),
        in_specs=vmem(1),
        out_specs=vmem(1)[0],
        compiler_params=PARAMS,
        cost_estimate=pl.CostEstimate(flops=10**5, bytes_accessed=300000, transcendentals=0),
        name="collect",
    )(rows)
    done = pl.pallas_call(
        sections_kernel,
        out_shape=jax.ShapeDtypeStruct((128, LANES), jnp.float32),
        in_specs=vmem(3),
        out_specs=vmem(1)[0],
        compiler_params=PARAMS,
        name="sections",
    )(own, halo, tables)
    back = lax.all_to_all(done.reshape(16, 8, LANES), ("lev", "px"), 0, 0, tiled=True)
    return pl.pallas_call(
        remap_kernel,
        out_shape=jax.ShapeDtypeStruct((2, 4, 8, LANES), jnp.float32),
        in_specs=vmem(2),
        out_specs=vmem(1)[0],
        compiler_params=PARAMS,
        name="remap",
    )(remap, back)


def solution(mesh):
    in_specs = (
        P("lev", None, "px", "py"),
        P("lev", "px", "py"),
        P("lev", "px", "py"),
        P("lev", "px", "py"),
        P(),
    )
    out_specs = P(None, "lev", "px", "py")
    return jax.shard_map(shards, mesh=mesh, in_specs=in_specs, out_specs=out_specs, check_vma=False)
```

```python
import functools

import jax
import jax.numpy as jnp
import numpy as np
from jax import lax
from jax.experimental import pallas as pl
from jax.experimental.pallas import tpu as pltpu
from jax.sharding import PartitionSpec as P

GLL_NODES = 4
LANES = 128
PARAMS = pltpu.CompilerParams(vmem_limit_bytes=8 * 1024 * 1024)
SLOT = 32
WINDOW = 96
HALO = 24

sentinel = 1e30
step_size = 0.1
section_weights = ((0.0, 1.0), (0.75, 0.25), (1.0 / 3.0, 2.0 / 3.0))


def derivative_table():
    points = np.array([-1.0, -(5.0 ** (-0.5)), 5.0 ** (-0.5), 1.0])
    number = points.shape[0]
    barycentric = np.array(
        [
            1.0
            / np.prod([points[outer] - points[inner] for inner in range(number) if inner != outer])
            for outer in range(number)
        ]
    )
    table = np.zeros((number, number))
    for outer in range(number):
        for inner in range(number):
            if inner != outer:
                table[outer, inner] = (
                    barycentric[inner] / barycentric[outer] / (points[outer] - points[inner])
                )
    for outer in range(number):
        table[outer, outer] = -np.sum(table[outer])
    return table


def rot(x, k):
    k = k % LANES
    return pltpu.roll(x, k, 1) if k else x


def lane_index():
    return lax.broadcasted_iota(jnp.int32, (8, LANES), 1)


def node_index():
    return lane_index() % GLL_NODES


def table_kernel(out_ref):
    table = derivative_table() * step_size
    source = lax.broadcasted_iota(jnp.int32, (LANES, LANES), 0)
    target = lax.broadcasted_iota(jnp.int32, (LANES, LANES), 1)
    place = (target % GLL_NODES) * GLL_NODES + source % GLL_NODES
    c = jnp.zeros((LANES, LANES), jnp.float32)
    for i in range(GLL_NODES):
        for j in range(GLL_NODES):
            c = jnp.where(place == i * GLL_NODES + j, jnp.float32(table[i, j]), c)
    c = jnp.where(source // GLL_NODES == target // GLL_NODES, c, 0.0)
    high = c.astype(jnp.bfloat16)
    out_ref[0] = high
    out_ref[1] = (c - high.astype(jnp.float32)).astype(jnp.bfloat16)


def pack_kernel(first_ref, t_ref, m_ref, x_ref, y_ref, out_ref):
    odd = lax.axis_index("py") % 2
    lane = lane_index()
    for half in range(2):
        shift = -SLOT * half
        turn = [HALO * u + (HALO - WINDOW) * half for u in range(4)]
        window = [(lane + LANES - turn[u]) % LANES < WINDOW for u in range(4)]
        piece = [rot(y_ref[0], WINDOW - SLOT * u + shift + turn[u]) for u in range(3)]
        mass = jnp.where(window[2], rot(m_ref[0], shift + turn[2]), piece[2])
        last = rot(y_ref[0], HALO + shift + turn[3])
        wind = jnp.where(window[3], rot(x_ref[0], shift + turn[3]), last)
        place = jnp.where(odd == 1, 1 - half, half)
        for q in range(4):
            for u in range(2):
                t = rot(t_ref[0, 2 * q + u], shift + turn[u])
                out_ref[2 * q + place, u] = jnp.where(window[u], t, piece[u])
            out_ref[2 * q + place, 2] = mass
            out_ref[2 * q + place, 3] = wind


def gathered(r_ref, u, r):
    return r_ref[pl.ds(u * 8 + r, 8, stride=32), :]


def works_left():
    return (lax.axis_index("px") + lax.axis_index("py")) % 2 == 0


def moved_lanes(x, left, if_left, if_right):
    return pltpu.roll(x, jnp.where(left, if_left % LANES, if_right % LANES), 1)


def edge_kernel(r_ref, out_ref):
    slot = lane_index() // HALO
    left = works_left()
    for r in range(8):
        unit = [gathered(r_ref, u, r) for u in range(4)]
        edge = jnp.where(left, unit[0], unit[3])
        for a in range(4):
            edge = jnp.where(slot == a, unit[a], edge)
        out_ref[r] = edge


def collect_kernel(r_ref, out_ref):
    lane = lane_index()
    left = works_left()
    for r in range(8):
        unit = [
            moved_lanes(gathered(r_ref, u, r), left, -HALO * u, WINDOW - HALO - HALO * u)
            for u in range(4)
        ]
        last = jnp.where(lane < 2 * SLOT, rot(unit[1], 2 * SLOT), rot(unit[2], 3 * SLOT))
        last = jnp.where(lane < SLOT, rot(unit[0], SLOT), last)
        for a in range(4):
            out_ref[a, r] = unit[a]
        out_ref[4, r] = last


def sections_kernel(own_ref, halo_ref, table_ref, out_ref):
    lane = lane_index()
    node = node_index()
    py = lax.axis_index("py")
    left = works_left()
    has_halo = (left & (py > 0)) | (~left & (py < lax.axis_size("py") - 1))
    exists = (lane < WINDOW) | has_halo
    inner_end = jnp.where(left, LANES, WINDOW + HALO)
    in_halo = (lane >= inner_end - HALO) & (lane < inner_end)
    rim_node = (node == 0) | (node == 3)
    partner = jnp.where(node == 0, lane - 1, jnp.where(node == 3, lane + 1, lane))
    partner = (partner + LANES) % LANES
    table = derivative_table() * step_size
    rows = range(8)

    def permuted(x, index):
        return jnp.take_along_axis(x, index, axis=1, mode="promise_in_bounds")

    def completed(a, fill):
        result = []
        for r in rows:
            halo = moved_lanes(halo_ref[r], left, LANES - HALO - HALO * a, WINDOW - HALO * a)
            halo = jnp.where(in_halo, halo, jnp.float32(fill))
            result.append(jnp.where(lane < WINDOW, own_ref[a, r], halo))
        return result

    def up(x):
        return pltpu.roll(x, 1, 0)

    def down(x):
        return pltpu.roll(x, 7, 0)

    def shared(f):
        f = list(f)
        first, last = f[0], f[7]
        f[0] = first + up(last)
        f[7] = last + down(first)
        f[3] = f[4] = f[3] + f[4]
        return [x + jnp.where(rim_node, permuted(x, partner), 0.0) for x in f]

    def extreme(f, op, missing):
        halves = []
        for e in range(2):
            x = op(op(f[4 * e], f[4 * e + 1]), op(f[4 * e + 2], f[4 * e + 3]))
            x = op(x, permuted(x, lane ^ 1))
            x = op(x, permuted(x, lane ^ 2))
            x = jnp.where(exists, x, missing)
            halves.append(op(op(x, rot(x, 4)), rot(x, -4)))
        zero, one = halves
        both = op(zero, one)
        return op(both, up(one)), op(both, down(zero))

    def slopes_x(f):
        outer, inner = f[0] - f[3], f[1] - f[2]
        even_part = (f[0] + f[3]) - (f[1] + f[2])
        result = [None] * 4
        for i in range(2):
            p = jnp.float32((table[i, 0] - table[i, 3]) / 2) * outer
            p = p + jnp.float32((table[i, 1] - table[i, 2]) / 2) * inner
            q = jnp.float32((table[i, 0] + table[i, 3]) / 2) * even_part
            result[i], result[3 - i] = p + q, p - q
        return result

    mass = completed(2, 1.0)
    wind_x = completed(3, 0.0)
    wind_y = completed(4, 0.0)
    inverse = [jnp.where(exists, 1.0 / jnp.where(exists, m, 1.0), 0.0) for m in shared(mass)]
    starts = [completed(tracer, 0.0) for tracer in range(2)]
    fields = list(starts)
    for share_start, share_new in section_weights:
        flux = jnp.concatenate([wind_y[r] * f[r] for f in fields for r in rows], axis=0)
        high = flux.astype(jnp.bfloat16)
        low = (flux - high.astype(jnp.float32)).astype(jnp.bfloat16)
        both = jnp.concatenate([high, low], axis=0)
        product = jnp.dot(both, table_ref[0], preferred_element_type=jnp.float32)
        small = jnp.dot(high, table_ref[1], preferred_element_type=jnp.float32)
        along_y = (product[128:] + small) + product[:128]
        lowers = [extreme(f, jnp.minimum, sentinel) for f in fields]
        uppers = [extreme(f, jnp.maximum, -sentinel) for f in fields]
        weighted = [[None] * 8, [None] * 8]
        for e in range(2):
            for t in range(2):
                field = fields[t]
                along_x = slopes_x([wind_x[4 * e + i] * field[4 * e + i] for i in range(4)])
                for i in range(4):
                    r = 4 * e + i
                    at = 64 * t + 8 * r
                    moved = field[r] - (along_x[i] + along_y[at : at + 8])
                    limited = jnp.minimum(jnp.maximum(moved, lowers[t][e]), uppers[t][e])
                    weighted[t][r] = mass[r] * limited
        summed = [shared(w) for w in weighted]
        fresh = [[None] * 8, [None] * 8]
        for r in rows:
            for t in range(2):
                value = summed[t][r] * inverse[r]
                if share_new != 1.0:
                    value = jnp.float32(share_new) * value
                if share_start:
                    value = jnp.float32(share_start) * starts[t][r] + value
                fresh[t][r] = value
        fields = fresh
    finished = fields
    for r in rows:
        low = moved_lanes(finished[0][r], left, 0, -SLOT)
        high = moved_lanes(finished[1][r], left, 2 * SLOT, SLOT)
        both = jnp.where(lane < 2 * SLOT, low, high)
        for m in range(2):
            out_ref[pl.ds(m * 64 + r, 8, stride=8), :] = both


def remap_kernel(remap_ref, x_ref, out_ref):
    base = lax.axis_index("lev") * 4
    odd = lax.axis_index("py") % 2
    low = lane_index() < LANES // 2
    weight = [[remap_ref[a : a + 1, b : b + 1] for b in range(2)] for a in range(2)]
    for q in range(2):
        first, second = [], []
        for level in range(2):
            left = x_ref[base + 2 * q + odd + 8 * level]
            right = x_ref[base + 2 * q + 1 - odd + 8 * level]
            first.append(jnp.where(low, left, rot(right, LANES // 2)))
            second.append(jnp.where(low, rot(left, LANES // 2), right))
        for a in range(2):
            out_ref[a, 2 * q] = weight[a][0] * first[0] + weight[a][1] * first[1]
            out_ref[a, 2 * q + 1] = weight[a][0] * second[0] + weight[a][1] * second[1]


def vmem(count):
    return [pl.BlockSpec(memory_space=pltpu.VMEM)] * count


def shards(tracer, node_mass, wind_x, wind_y, remap):
    count = lax.axis_size("py")
    tables = pl.pallas_call(
        table_kernel,
        out_shape=jax.ShapeDtypeStruct((2, LANES, LANES), jnp.bfloat16),
        out_specs=vmem(1)[0],
        compiler_params=PARAMS,
        cost_estimate=pl.CostEstimate(flops=10**10, bytes_accessed=10**7, transcendentals=0),
        name="tables",
    )()
    packed = pl.pallas_call(
        pack_kernel,
        out_shape=jax.ShapeDtypeStruct((8, 4, 8, LANES), jnp.float32),
        in_specs=vmem(5),
        out_specs=vmem(1)[0],
        compiler_params=PARAMS,
        name="pack",
    )(tables, tracer, node_mass, wind_x, wind_y)
    rows = lax.all_to_all(packed, "px", 0, 0, tiled=True).reshape(256, LANES)
    edge = pl.pallas_call(
        edge_kernel,
        out_shape=jax.ShapeDtypeStruct((8, 8, LANES), jnp.float32),
        in_specs=vmem(1),
        out_specs=vmem(1)[0],
        compiler_params=PARAMS,
        name="edge",
    )(rows)
    pairs = []
    for px in range(lax.axis_size("px")):
        for py in range(2 - px % 2, count, 2):
            a = px * count + py
            pairs += [(a, a - 1), (a - 1, a)]
    halo = lax.ppermute(edge, ("px", "py"), pairs)
    own = pl.pallas_call(
        collect_kernel,
        out_shape=jax.ShapeDtypeStruct((5, 8, 8, LANES), jnp.float32),
        in_specs=vmem(1),
        out_specs=vmem(1)[0],
        compiler_params=PARAMS,
        cost_estimate=pl.CostEstimate(flops=10**5, bytes_accessed=300000, transcendentals=0),
        name="collect",
    )(rows)
    done = pl.pallas_call(
        sections_kernel,
        out_shape=jax.ShapeDtypeStruct((128, LANES), jnp.float32),
        in_specs=vmem(3),
        out_specs=vmem(1)[0],
        compiler_params=PARAMS,
        name="sections",
    )(own, halo, tables)
    back = lax.all_to_all(done.reshape(16, 8, LANES), ("lev", "px"), 0, 0, tiled=True)
    return pl.pallas_call(
        remap_kernel,
        out_shape=jax.ShapeDtypeStruct((2, 4, 8, LANES), jnp.float32),
        in_specs=vmem(2),
        out_specs=vmem(1)[0],
        compiler_params=PARAMS,
        name="remap",
    )(remap, back)


def solution(mesh):
    in_specs = (
        P("lev", None, "px", "py"),
        P("lev", "px", "py"),
        P("lev", "px", "py"),
        P("lev", "px", "py"),
        P(),
    )
    out_specs = P(None, "lev", "px", "py")
    return jax.shard_map(shards, mesh=mesh, in_specs=in_specs, out_specs=out_specs, check_vma=False)
```

```python
import functools

import jax
import jax.numpy as jnp
import numpy as np
from jax import lax
from jax.experimental import pallas as pl
from jax.experimental.pallas import tpu as pltpu
from jax.sharding import PartitionSpec as P

GLL_NODES = 4
LANES = 128
PARAMS = pltpu.CompilerParams(vmem_limit_bytes=8 * 1024 * 1024)
SCHEDULED = pltpu.CompilerParams(
    vmem_limit_bytes=8 * 1024 * 1024
)
SLOT = 32
WINDOW = 96
HALO = 24

sentinel = 1e30
step_size = 0.1
section_weights = ((0.0, 1.0), (0.75, 0.25), (1.0 / 3.0, 2.0 / 3.0))


def derivative_table():
    points = np.array([-1.0, -(5.0 ** (-0.5)), 5.0 ** (-0.5), 1.0])
    number = points.shape[0]
    barycentric = np.array(
        [
            1.0
            / np.prod([points[outer] - points[inner] for inner in range(number) if inner != outer])
            for outer in range(number)
        ]
    )
    table = np.zeros((number, number))
    for outer in range(number):
        for inner in range(number):
            if inner != outer:
                table[outer, inner] = (
                    barycentric[inner] / barycentric[outer] / (points[outer] - points[inner])
                )
    for outer in range(number):
        table[outer, outer] = -np.sum(table[outer])
    return table


def rot(x, k):
    k = k % LANES
    return pltpu.roll(x, k, 1) if k else x


def lane_index():
    return lax.broadcasted_iota(jnp.int32, (8, LANES), 1)


def node_index():
    return lane_index() % GLL_NODES


def table_kernel(out_ref):
    table = derivative_table() * step_size
    source = lax.broadcasted_iota(jnp.int32, (LANES, LANES), 0)
    target = lax.broadcasted_iota(jnp.int32, (LANES, LANES), 1)
    place = (target % GLL_NODES) * GLL_NODES + source % GLL_NODES
    c = jnp.zeros((LANES, LANES), jnp.float32)
    for i in range(GLL_NODES):
        for j in range(GLL_NODES):
            c = jnp.where(place == i * GLL_NODES + j, jnp.float32(table[i, j]), c)
    c = jnp.where(source // GLL_NODES == target // GLL_NODES, c, 0.0)
    high = c.astype(jnp.bfloat16)
    out_ref[0] = high
    out_ref[1] = (c - high.astype(jnp.float32)).astype(jnp.bfloat16)


def pack_kernel(first_ref, t_ref, m_ref, x_ref, y_ref, out_ref):
    odd = lax.axis_index("py") % 2
    lane = lane_index()
    for half in range(2):
        shift = -SLOT * half
        turn = [HALO * u + (HALO - WINDOW) * half for u in range(4)]
        window = [(lane + LANES - turn[u]) % LANES < WINDOW for u in range(4)]
        piece = [rot(y_ref[0], WINDOW - SLOT * u + shift + turn[u]) for u in range(3)]
        mass = jnp.where(window[2], rot(m_ref[0], shift + turn[2]), piece[2])
        last = rot(y_ref[0], HALO + shift + turn[3])
        wind = jnp.where(window[3], rot(x_ref[0], shift + turn[3]), last)
        place = jnp.where(odd == 1, 1 - half, half)
        for q in range(4):
            for u in range(2):
                t = rot(t_ref[0, 2 * q + u], shift + turn[u])
                out_ref[2 * q + place, u] = jnp.where(window[u], t, piece[u])
            out_ref[2 * q + place, 2] = mass
            out_ref[2 * q + place, 3] = wind


def gathered(r_ref, u, r):
    return r_ref[pl.ds(u * 8 + r, 8, stride=32), :]


def works_left():
    return (lax.axis_index("px") + lax.axis_index("py")) % 2 == 0


def moved_lanes(x, left, if_left, if_right):
    return pltpu.roll(x, jnp.where(left, if_left % LANES, if_right % LANES), 1)


def edge_kernel(r_ref, out_ref):
    slot = lane_index() // HALO
    left = works_left()
    for r in range(8):
        unit = [gathered(r_ref, u, r) for u in range(4)]
        edge = jnp.where(left, unit[0], unit[3])
        for a in range(4):
            edge = jnp.where(slot == a, unit[a], edge)
        out_ref[r] = edge


def collect_kernel(r_ref, out_ref):
    lane = lane_index()
    left = works_left()
    for r in range(8):
        unit = [
            moved_lanes(gathered(r_ref, u, r), left, -HALO * u, WINDOW - HALO - HALO * u)
            for u in range(4)
        ]
        last = jnp.where(lane < 2 * SLOT, rot(unit[1], 2 * SLOT), rot(unit[2], 3 * SLOT))
        last = jnp.where(lane < SLOT, rot(unit[0], SLOT), last)
        for a in range(4):
            out_ref[a, r] = unit[a]
        out_ref[4, r] = last


def sections_kernel(own_ref, halo_ref, table_ref, out_ref):
    lane = lane_index()
    node = node_index()
    py = lax.axis_index("py")
    left = works_left()
    has_halo = (left & (py > 0)) | (~left & (py < lax.axis_size("py") - 1))
    exists = (lane < WINDOW) | has_halo
    inner_end = jnp.where(left, LANES, WINDOW + HALO)
    in_halo = (lane >= inner_end - HALO) & (lane < inner_end)
    rim_node = (node == 0) | (node == 3)
    partner = jnp.where(node == 0, lane - 1, jnp.where(node == 3, lane + 1, lane))
    partner = (partner + LANES) % LANES
    table = derivative_table() * step_size
    rows = range(8)

    def permuted(x, index):
        return jnp.take_along_axis(x, index, axis=1, mode="promise_in_bounds")

    def completed(a, fill):
        result = []
        for r in rows:
            halo = moved_lanes(halo_ref[r], left, LANES - HALO - HALO * a, WINDOW - HALO * a)
            halo = jnp.where(in_halo, halo, jnp.float32(fill))
            result.append(jnp.where(lane < WINDOW, own_ref[a, r], halo))
        return result

    def up(x):
        return pltpu.roll(x, 1, 0)

    def down(x):
        return pltpu.roll(x, 7, 0)

    def shared(f):
        f = list(f)
        first, last = f[0], f[7]
        f[0] = first + up(last)
        f[7] = last + down(first)
        f[3] = f[4] = f[3] + f[4]
        return [x + jnp.where(rim_node, permuted(x, partner), 0.0) for x in f]

    def extreme(f, op, missing):
        halves = []
        for e in range(2):
            x = op(op(f[4 * e], f[4 * e + 1]), op(f[4 * e + 2], f[4 * e + 3]))
            x = op(x, permuted(x, lane ^ 1))
            x = op(x, permuted(x, lane ^ 2))
            x = jnp.where(exists, x, missing)
            halves.append(op(op(x, rot(x, 4)), rot(x, -4)))
        zero, one = halves
        both = op(zero, one)
        return op(both, up(one)), op(both, down(zero))

    def slopes_x(f):
        outer, inner = f[0] - f[3], f[1] - f[2]
        even_part = (f[0] + f[3]) - (f[1] + f[2])
        result = [None] * 4
        for i in range(2):
            p = jnp.float32((table[i, 0] - table[i, 3]) / 2) * outer
            p = p + jnp.float32((table[i, 1] - table[i, 2]) / 2) * inner
            q = jnp.float32((table[i, 0] + table[i, 3]) / 2) * even_part
            result[i], result[3 - i] = p + q, p - q
        return result

    mass = completed(2, 1.0)
    wind_x = completed(3, 0.0)
    wind_y = completed(4, 0.0)
    inverse = [jnp.where(exists, 1.0 / jnp.where(exists, m, 1.0), 0.0) for m in shared(mass)]
    starts = [completed(tracer, 0.0) for tracer in range(2)]
    fields = list(starts)
    for share_start, share_new in section_weights:
        flux = jnp.concatenate([wind_y[r] * f[r] for f in fields for r in rows], axis=0)
        high = flux.astype(jnp.bfloat16)
        low = (flux - high.astype(jnp.float32)).astype(jnp.bfloat16)
        both = jnp.concatenate([high, low], axis=0)
        product = jnp.dot(both, table_ref[0], preferred_element_type=jnp.float32)
        small = jnp.dot(high, table_ref[1], preferred_element_type=jnp.float32)
        along_y = (product[128:] + small) + product[:128]
        lowers = [extreme(f, jnp.minimum, sentinel) for f in fields]
        uppers = [extreme(f, jnp.maximum, -sentinel) for f in fields]
        weighted = [[None] * 8, [None] * 8]
        for e in range(2):
            for t in range(2):
                field = fields[t]
                along_x = slopes_x([wind_x[4 * e + i] * field[4 * e + i] for i in range(4)])
                for i in range(4):
                    r = 4 * e + i
                    at = 64 * t + 8 * r
                    moved = field[r] - (along_x[i] + along_y[at : at + 8])
                    limited = jnp.minimum(jnp.maximum(moved, lowers[t][e]), uppers[t][e])
                    weighted[t][r] = mass[r] * limited
        summed = [shared(w) for w in weighted]
        fresh = [[None] * 8, [None] * 8]
        for r in rows:
            for t in range(2):
                value = summed[t][r] * inverse[r]
                if share_new != 1.0:
                    value = jnp.float32(share_new) * value
                if share_start:
                    value = jnp.float32(share_start) * starts[t][r] + value
                fresh[t][r] = value
        fields = fresh
    finished = fields
    for r in rows:
        low = moved_lanes(finished[0][r], left, 0, -SLOT)
        high = moved_lanes(finished[1][r], left, 2 * SLOT, SLOT)
        both = jnp.where(lane < 2 * SLOT, low, high)
        for m in range(2):
            out_ref[pl.ds(m * 64 + r, 8, stride=8), :] = both


def remap_kernel(remap_ref, x_ref, out_ref):
    base = lax.axis_index("lev") * 4
    odd = lax.axis_index("py") % 2
    low = lane_index() < LANES // 2
    weight = [[remap_ref[a : a + 1, b : b + 1] for b in range(2)] for a in range(2)]
    for q in range(2):
        first, second = [], []
        for level in range(2):
            left = x_ref[base + 2 * q + odd + 8 * level]
            right = x_ref[base + 2 * q + 1 - odd + 8 * level]
            first.append(jnp.where(low, left, rot(right, LANES // 2)))
            second.append(jnp.where(low, rot(left, LANES // 2), right))
        for a in range(2):
            out_ref[a, 2 * q] = weight[a][0] * first[0] + weight[a][1] * first[1]
            out_ref[a, 2 * q + 1] = weight[a][0] * second[0] + weight[a][1] * second[1]


def vmem(count):
    return [pl.BlockSpec(memory_space=pltpu.VMEM)] * count


def shards(tracer, node_mass, wind_x, wind_y, remap):
    count = lax.axis_size("py")
    tables = pl.pallas_call(
        table_kernel,
        out_shape=jax.ShapeDtypeStruct((2, LANES, LANES), jnp.bfloat16),
        out_specs=vmem(1)[0],
        compiler_params=PARAMS,
        cost_estimate=pl.CostEstimate(flops=10**10, bytes_accessed=10**7, transcendentals=0),
        name="tables",
    )()
    packed = pl.pallas_call(
        pack_kernel,
        out_shape=jax.ShapeDtypeStruct((8, 4, 8, LANES), jnp.float32),
        in_specs=vmem(5),
        out_specs=vmem(1)[0],
        compiler_params=PARAMS,
        name="pack",
    )(tables, tracer, node_mass, wind_x, wind_y)
    rows = lax.all_to_all(packed, "px", 0, 0, tiled=True).reshape(256, LANES)
    edge = pl.pallas_call(
        edge_kernel,
        out_shape=jax.ShapeDtypeStruct((8, 8, LANES), jnp.float32),
        in_specs=vmem(1),
        out_specs=vmem(1)[0],
        compiler_params=SCHEDULED,
        name="edge",
    )(rows)
    pairs = []
    for px in range(lax.axis_size("px")):
        for py in range(2 - px % 2, count, 2):
            a = px * count + py
            pairs += [(a, a - 1), (a - 1, a)]
    halo = lax.ppermute(edge, ("px", "py"), pairs)
    own = pl.pallas_call(
        collect_kernel,
        out_shape=jax.ShapeDtypeStruct((5, 8, 8, LANES), jnp.float32),
        in_specs=vmem(1),
        out_specs=vmem(1)[0],
        compiler_params=PARAMS,
        cost_estimate=pl.CostEstimate(flops=10**5, bytes_accessed=300000, transcendentals=0),
        name="collect",
    )(rows)
    done = pl.pallas_call(
        sections_kernel,
        out_shape=jax.ShapeDtypeStruct((128, LANES), jnp.float32),
        in_specs=vmem(3),
        out_specs=vmem(1)[0],
        compiler_params=SCHEDULED,
        name="sections",
    )(own, halo, tables)
    back = lax.all_to_all(done.reshape(16, 8, LANES), ("lev", "px"), 0, 0, tiled=True)
    return pl.pallas_call(
        remap_kernel,
        out_shape=jax.ShapeDtypeStruct((2, 4, 8, LANES), jnp.float32),
        in_specs=vmem(2),
        out_specs=vmem(1)[0],
        compiler_params=PARAMS,
        name="remap",
    )(remap, back)


def solution(mesh):
    in_specs = (
        P("lev", None, "px", "py"),
        P("lev", "px", "py"),
        P("lev", "px", "py"),
        P("lev", "px", "py"),
        P(),
    )
    out_specs = P(None, "lev", "px", "py")
    return jax.shard_map(shards, mesh=mesh, in_specs=in_specs, out_specs=out_specs, check_vma=False)
```

```python
import functools

import jax
import jax.numpy as jnp
import numpy as np
from jax import lax
from jax.experimental import pallas as pl
from jax.experimental.pallas import tpu as pltpu
from jax.sharding import PartitionSpec as P

GLL_NODES = 4
LANES = 128
PARAMS = pltpu.CompilerParams(vmem_limit_bytes=8 * 1024 * 1024)
SLOT = 32
WINDOW = 96
HALO = 24

sentinel = 1e30
step_size = 0.1
section_weights = ((0.0, 1.0), (0.75, 0.25), (1.0 / 3.0, 2.0 / 3.0))


def derivative_table():
    points = np.array([-1.0, -(5.0 ** (-0.5)), 5.0 ** (-0.5), 1.0])
    number = points.shape[0]
    barycentric = np.array(
        [
            1.0
            / np.prod([points[outer] - points[inner] for inner in range(number) if inner != outer])
            for outer in range(number)
        ]
    )
    table = np.zeros((number, number))
    for outer in range(number):
        for inner in range(number):
            if inner != outer:
                table[outer, inner] = (
                    barycentric[inner] / barycentric[outer] / (points[outer] - points[inner])
                )
    for outer in range(number):
        table[outer, outer] = -np.sum(table[outer])
    return table


def rot(x, k):
    k = k % LANES
    return pltpu.roll(x, k, 1) if k else x


def lane_index():
    return lax.broadcasted_iota(jnp.int32, (8, LANES), 1)


def node_index():
    return lane_index() % GLL_NODES


def table_kernel(out_ref):
    table = derivative_table() * step_size
    source = lax.broadcasted_iota(jnp.int32, (LANES, LANES), 0)
    target = lax.broadcasted_iota(jnp.int32, (LANES, LANES), 1)
    place = (target % GLL_NODES) * GLL_NODES + source % GLL_NODES
    c = jnp.zeros((LANES, LANES), jnp.float32)
    for i in range(GLL_NODES):
        for j in range(GLL_NODES):
            c = jnp.where(place == i * GLL_NODES + j, jnp.float32(table[i, j]), c)
    c = jnp.where(source // GLL_NODES == target // GLL_NODES, c, 0.0)
    high = c.astype(jnp.bfloat16)
    out_ref[0] = high
    out_ref[1] = (c - high.astype(jnp.float32)).astype(jnp.bfloat16)


def pack_kernel(first_ref, t_ref, m_ref, x_ref, y_ref, out_ref):
    odd = lax.axis_index("py") % 2
    lane = lane_index()
    for half in range(2):
        shift = -SLOT * half
        turn = [HALO * u + (HALO - WINDOW) * half for u in range(4)]
        window = [(lane + LANES - turn[u]) % LANES < WINDOW for u in range(4)]
        piece = [rot(y_ref[0], WINDOW - SLOT * u + shift + turn[u]) for u in range(3)]
        mass = jnp.where(window[2], rot(m_ref[0], shift + turn[2]), piece[2])
        last = rot(y_ref[0], HALO + shift + turn[3])
        wind = jnp.where(window[3], rot(x_ref[0], shift + turn[3]), last)
        place = jnp.where(odd == 1, 1 - half, half)
        for q in range(4):
            for u in range(2):
                t = rot(t_ref[0, 2 * q + u], shift + turn[u])
                out_ref[2 * q + place, u] = jnp.where(window[u], t, piece[u])
            out_ref[2 * q + place, 2] = mass
            out_ref[2 * q + place, 3] = wind


def gathered(r_ref, u, r):
    return r_ref[pl.ds(u * 8 + r, 8, stride=32), :]


def works_left():
    return (lax.axis_index("px") + lax.axis_index("py")) % 2 == 0


def moved_lanes(x, left, if_left, if_right):
    return pltpu.roll(x, jnp.where(left, if_left % LANES, if_right % LANES), 1)


def edge_kernel(r_ref, out_ref):
    slot = lane_index() // HALO
    left = works_left()
    for r in range(8):
        unit = [gathered(r_ref, u, r) for u in range(4)]
        edge = jnp.where(left, unit[0], unit[3])
        for a in range(4):
            edge = jnp.where(slot == a, unit[a], edge)
        out_ref[r] = edge


def collect_kernel(r_ref, out_ref):
    lane = lane_index()
    left = works_left()
    for r in range(8):
        unit = [
            moved_lanes(gathered(r_ref, u, r), left, -HALO * u, WINDOW - HALO - HALO * u)
            for u in range(4)
        ]
        last = jnp.where(lane < 2 * SLOT, rot(unit[1], 2 * SLOT), rot(unit[2], 3 * SLOT))
        last = jnp.where(lane < SLOT, rot(unit[0], SLOT), last)
        for a in range(4):
            out_ref[a, r] = unit[a]
        out_ref[4, r] = last


def sections_kernel(own_ref, halo_ref, table_ref, out_ref):
    lane = lane_index()
    node = node_index()
    py = lax.axis_index("py")
    left = works_left()
    has_halo = (left & (py > 0)) | (~left & (py < lax.axis_size("py") - 1))
    exists = (lane < WINDOW) | has_halo
    inner_end = jnp.where(left, LANES, WINDOW + HALO)
    in_halo = (lane >= inner_end - HALO) & (lane < inner_end)
    rim_node = (node == 0) | (node == 3)
    partner = jnp.where(node == 0, lane - 1, jnp.where(node == 3, lane + 1, lane))
    partner = (partner + LANES) % LANES
    table = derivative_table() * step_size
    rows = range(8)

    def permuted(x, index):
        return jnp.take_along_axis(x, index, axis=1, mode="promise_in_bounds")

    def completed(a, fill):
        result = []
        for r in rows:
            halo = moved_lanes(halo_ref[r], left, LANES - HALO - HALO * a, WINDOW - HALO * a)
            halo = jnp.where(in_halo, halo, jnp.float32(fill))
            result.append(jnp.where(lane < WINDOW, own_ref[a, r], halo))
        return result

    def up(x):
        return pltpu.roll(x, 1, 0)

    def down(x):
        return pltpu.roll(x, 7, 0)

    def shared(f):
        f = list(f)
        first, last = f[0], f[7]
        f[0] = first + up(last)
        f[7] = last + down(first)
        f[3] = f[4] = f[3] + f[4]
        return [x + jnp.where(rim_node, permuted(x, partner), 0.0) for x in f]

    def extreme(f, op, missing):
        halves = []
        for e in range(2):
            x = op(op(f[4 * e], f[4 * e + 1]), op(f[4 * e + 2], f[4 * e + 3]))
            x = op(x, permuted(x, lane ^ 1))
            x = op(x, permuted(x, lane ^ 2))
            x = jnp.where(exists, x, missing)
            halves.append(op(op(x, rot(x, 4)), rot(x, -4)))
        zero, one = halves
        both = op(zero, one)
        return op(both, up(one)), op(both, down(zero))

    def slopes_x(f):
        outer, inner = f[0] - f[3], f[1] - f[2]
        even_part = (f[0] + f[3]) - (f[1] + f[2])
        result = [None] * 4
        for i in range(2):
            p = jnp.float32((table[i, 0] - table[i, 3]) / 2) * outer
            p = p + jnp.float32((table[i, 1] - table[i, 2]) / 2) * inner
            q = jnp.float32((table[i, 0] + table[i, 3]) / 2) * even_part
            result[i], result[3 - i] = p + q, p - q
        return result

    mass = completed(2, 1.0)
    wind_x = completed(3, 0.0)
    wind_y = completed(4, 0.0)
    inverse = [jnp.where(exists, 1.0 / jnp.where(exists, m, 1.0), 0.0) for m in shared(mass)]
    starts = [completed(tracer, 0.0) for tracer in range(2)]
    fields = list(starts)
    for share_start, share_new in section_weights:
        flux = jnp.concatenate([wind_y[r] * f[r] for f in fields for r in rows], axis=0)
        high = flux.astype(jnp.bfloat16)
        low = (flux - high.astype(jnp.float32)).astype(jnp.bfloat16)
        both = jnp.concatenate([high, low], axis=0)
        product = jnp.dot(both, table_ref[0], preferred_element_type=jnp.float32)
        small = jnp.dot(high, table_ref[1], preferred_element_type=jnp.float32)
        along_y = (product[128:] + small) + product[:128]
        lowers = [extreme(f, jnp.minimum, sentinel) for f in fields]
        uppers = [extreme(f, jnp.maximum, -sentinel) for f in fields]
        weighted = [[None] * 8, [None] * 8]
        for e in range(2):
            for t in range(2):
                field = fields[t]
                along_x = slopes_x([wind_x[4 * e + i] * field[4 * e + i] for i in range(4)])
                for i in range(4):
                    r = 4 * e + i
                    at = 64 * t + 8 * r
                    moved = field[r] - (along_x[i] + along_y[at : at + 8])
                    limited = jnp.minimum(jnp.maximum(moved, lowers[t][e]), uppers[t][e])
                    weighted[t][r] = mass[r] * limited
        summed = [shared(w) for w in weighted]
        fresh = [[None] * 8, [None] * 8]
        for r in rows:
            for t in range(2):
                value = summed[t][r] * inverse[r]
                if share_new != 1.0:
                    value = jnp.float32(share_new) * value
                if share_start:
                    value = jnp.float32(share_start) * starts[t][r] + value
                fresh[t][r] = value
        fields = fresh
    finished = fields
    for r in rows:
        low = moved_lanes(finished[0][r], left, 0, -SLOT)
        high = moved_lanes(finished[1][r], left, 2 * SLOT, SLOT)
        both = jnp.where(lane < 2 * SLOT, low, high)
        for m in range(2):
            out_ref[pl.ds(m * 64 + r, 8, stride=8), :] = both


def remap_kernel(remap_ref, x_ref, out_ref):
    base = lax.axis_index("lev") * 4
    odd = lax.axis_index("py") % 2
    low = lane_index() < LANES // 2
    weight = [[remap_ref[a : a + 1, b : b + 1] for b in range(2)] for a in range(2)]
    for q in range(2):
        first, second = [], []
        for level in range(2):
            left = x_ref[base + 2 * q + odd + 8 * level]
            right = x_ref[base + 2 * q + 1 - odd + 8 * level]
            first.append(jnp.where(low, left, rot(right, LANES // 2)))
            second.append(jnp.where(low, rot(left, LANES // 2), right))
        for a in range(2):
            out_ref[a, 2 * q] = weight[a][0] * first[0] + weight[a][1] * first[1]
            out_ref[a, 2 * q + 1] = weight[a][0] * second[0] + weight[a][1] * second[1]


def vmem(count):
    return [pl.BlockSpec(memory_space=pltpu.VMEM)] * count


def shards(tracer, node_mass, wind_x, wind_y, remap):
    count = lax.axis_size("py")
    tables = pl.pallas_call(
        table_kernel,
        out_shape=jax.ShapeDtypeStruct((2, LANES, LANES), jnp.bfloat16),
        out_specs=vmem(1)[0],
        compiler_params=PARAMS,
        cost_estimate=pl.CostEstimate(flops=10**10, bytes_accessed=10**7, transcendentals=0),
        name="tables",
    )()
    packed = pl.pallas_call(
        pack_kernel,
        out_shape=jax.ShapeDtypeStruct((8, 4, 8, LANES), jnp.float32),
        in_specs=vmem(5),
        out_specs=vmem(1)[0],
        compiler_params=PARAMS,
        name="pack",
    )(tables, tracer, node_mass, wind_x, wind_y)
    rows = lax.all_to_all(packed, "px", 0, 0, tiled=True).reshape(256, LANES)
    edge = pl.pallas_call(
        edge_kernel,
        out_shape=jax.ShapeDtypeStruct((8, 8, LANES), jnp.float32),
        in_specs=vmem(1),
        out_specs=vmem(1)[0],
        compiler_params=PARAMS,
        name="edge",
    )(rows)
    pairs = []
    for px in range(lax.axis_size("px")):
        for py in range(2 - px % 2, count, 2):
            a = px * count + py
            pairs += [(a, a - 1), (a - 1, a)]
    halo = lax.ppermute(edge, ("px", "py"), pairs)
    own = pl.pallas_call(
        collect_kernel,
        out_shape=jax.ShapeDtypeStruct((5, 8, 8, LANES), jnp.float32),
        in_specs=vmem(1),
        out_specs=vmem(1)[0],
        compiler_params=PARAMS,
        cost_estimate=pl.CostEstimate(flops=10**5, bytes_accessed=300000, transcendentals=0),
        name="collect",
    )(rows)
    done = pl.pallas_call(
        sections_kernel,
        out_shape=jax.ShapeDtypeStruct((128, LANES), jnp.float32),
        in_specs=vmem(3),
        out_specs=vmem(1)[0],
        compiler_params=pltpu.CompilerParams(vmem_limit_bytes=8 * 1024 * 1024),
        name="sections",
    )(own, halo, tables)
    back = lax.all_to_all(done.reshape(16, 8, LANES), ("lev", "px"), 0, 0, tiled=True)
    return pl.pallas_call(
        remap_kernel,
        out_shape=jax.ShapeDtypeStruct((2, 4, 8, LANES), jnp.float32),
        in_specs=vmem(2),
        out_specs=vmem(1)[0],
        compiler_params=PARAMS,
        name="remap",
    )(remap, back)


def solution(mesh):
    in_specs = (
        P("lev", None, "px", "py"),
        P("lev", "px", "py"),
        P("lev", "px", "py"),
        P("lev", "px", "py"),
        P(),
    )
    out_specs = P(None, "lev", "px", "py")
    return jax.shard_map(shards, mesh=mesh, in_specs=in_specs, out_specs=out_specs, check_vma=False)
```
